32 devices in a mesh: group: 2 (over x), ctx: 8 (over z, y), exp: 2 (over core).
Axes of the slice: x: 2, y: 2, z: 4, core: 2. Of those that a mesh axis runs over, the one named last changes fastest.
Arguments:
- prompt_query: bfloat16 [2, 2, 2048, 2048], P('group', 'exp', 'ctx'), may hold values from -6 to 6
- prompt_keys: bfloat16 [2, 2, 2048, 256], P('group', 'exp', 'ctx'), may hold values from -6 to 6
- prompt_values: bfloat16 [2, 2, 2048, 256], P('group', 'exp', 'ctx'), may hold values from -24 to 24
- lengths: int32 [2, 2], P(None, 'exp'), may hold values from 1025 to 2048
- decode_query: bfloat16 [2, 2, 128, 2048], P('group', 'exp', None, 'ctx'), may hold values from -6 to 6
- fresh_keys: bfloat16 [2, 2, 128, 256], P('group', 'exp'), may hold values from -6 to 6
- fresh_values: bfloat16 [2, 2, 128, 256], P('group', 'exp'), may hold values from -24 to 24
- x_dec: bfloat16 [2, 2, 128, 2048], P('group', 'exp', 'ctx'), may hold values from -0.59765625 to 0.59765625
- w_out: bfloat16 [2048, 2048], P('ctx'), may hold values from -0.125 to 0.125
- norm_gain: bfloat16 [2048], replicated, may hold values from 0.5 to 1.5
- w_gate_up: bfloat16 [16, 2048, 1536], P(('ctx', 'exp')), may hold values from -0.125 to 0.125
- w_down: bfloat16 [16, 768, 2048], P(('ctx', 'exp')), may hold values from -0.21875 to 0.21875
- expert_ids: int32 [2, 2, 128, 8], P('group', 'exp', 'ctx'), may hold values from 0 to 15, all different within a row; in each aligned block of 16 rows (0 to 15, 16 to 31, ..., all dimensions but the last counted through in order) at most 16 rows name the same one
- gate_weights: float32 [2, 2, 128, 8], P('group', 'exp', 'ctx'), may hold values from 0.1 to 1
Outputs:
- prompt_attention: bfloat16 [2, 2, 2048, 2048], P('group', 'exp', 'ctx')
- out_dec: bfloat16 [2, 2, 128, 2048], P('group', 'exp', 'ctx')
The draws below stay inside these ranges and needn't reach their ends.
Inputs may be any that keep to these rules, and one draw needn't show every extreme that they name: `expert_ids`: the 8 experts of a row differ; among the rows of one device no expert is named more than 16 times.
All inputs are finite; a program needn't handle non-finite values.
Results may differ from the reference program's by a relative error of at most 0.025.
Values may be sent and summed in bfloat16 or wider, within the bound.
A program may use at most 128 MiB of HBM per device.

```python
import math
import jax
import jax.numpy as jnp
import numpy as np
from jax import lax

D = 2048
FF = 768
HEAD_SIZE = 128
QUERY_HEADS = 16
KEY_VALUE_HEADS = 2
TOP = 8
ROWS_DEV = 16
PROMPT_SLOTS = 2048
DECODE_REQUESTS = 128
EXPERTS = 16
CAP = 16
N_CTX = 8
N_EXP = 2


def bare_values(key, shape):
    return jnp.clip(jax.random.normal(key, shape, jnp.float32), -6.0, 6.0)


def draw_prompt_query(key, part):
    value_tensor = bare_values(jax.random.fold_in(key, 11), (2, N_EXP, PROMPT_SLOTS, QUERY_HEADS, HEAD_SIZE))
    return value_tensor.reshape(2, N_EXP, PROMPT_SLOTS, QUERY_HEADS * HEAD_SIZE).astype(jnp.bfloat16)


def draw_prompt_keys(key, part):
    value_tensor = bare_values(jax.random.fold_in(key, 13), (2, N_EXP, PROMPT_SLOTS, KEY_VALUE_HEADS, HEAD_SIZE))
    return value_tensor.reshape(2, N_EXP, PROMPT_SLOTS, KEY_VALUE_HEADS * HEAD_SIZE).astype(jnp.bfloat16)


def draw_decode_query(key, part):
    value_tensor = bare_values(jax.random.fold_in(key, 17), (2, N_EXP, DECODE_REQUESTS, QUERY_HEADS, HEAD_SIZE))
    return value_tensor.reshape(2, N_EXP, DECODE_REQUESTS, QUERY_HEADS * HEAD_SIZE).astype(jnp.bfloat16)


def touch_ends(drawn, stream_key, least, largest):
    shape = drawn.shape
    spot = [jax.random.randint(jax.random.fold_in(stream_key, axis), (), 0, shape[axis]) for axis in range(len(shape))]
    drawn = drawn.at[tuple(spot)].set(least)
    longest = shape.index(max(shape))
    spot[longest] = (spot[longest] + 1) % shape[longest]
    return drawn.at[tuple(spot)].set(largest)


def block_scale(key, extent, shards, low, largest):
    def one(position, shards_of):
        heights = jax.random.uniform(jax.random.fold_in(jax.random.fold_in(key, 6), position), (shards_of,), jnp.float32, low / len(shards), largest / len(shards))
        return jnp.repeat(jnp.exp(heights), extent[position] // shards_of).reshape((-1,) + (1,) * (len(extent) - position - 1))

    gain = one(*shards[0])
    for cut in shards[1:]:
        gain = gain * one(*cut)
    return gain


def assign_block(stream_key, own, number, rows, count, top, most, lean):
    order = jax.random.permutation(stream_key, count)
    heavy_load, usual = load_shares(count, rows * top, most, lean, True), load_shares(count, rows * top, most, lean, False)
    places = jnp.arange(count)

    def named(tallies, turn):
        used = int((tallies > 0).sum())
        fixed = max(1, used // 4)
        passed = fixed + (places - fixed + turn * (used - fixed)) % max(1, count - fixed)
        return jnp.zeros((count,), jnp.int32).at[order[jnp.where(places < fixed, places, passed)]].set(jnp.asarray(tallies, jnp.int32))

    tallies = jnp.where(number % 4 == 0, named(heavy_load, number // 4), named(usual, number - number // 4 - 1))
    mixed = jax.random.permutation(jax.random.fold_in(own, 3), count)
    giver, taker = mixed[0:count // 2 * 2:2], mixed[1:count // 2 * 2:2]
    slack = jnp.minimum(tallies[giver] - 1, most - tallies[taker]) // 2
    slack = jnp.where((giver == order[0]) | (taker == order[0]) | (tallies[taker] == 0), 0, jnp.maximum(slack, 0))
    passed = jax.random.randint(jax.random.fold_in(own, 4), (count // 2,), 0, 1 << 20) % (slack + 1)
    tallies = tallies.at[giver].add(-passed).at[taker].add(passed)
    labels = jnp.searchsorted(jnp.cumsum(tallies), jnp.arange(rows * top), side="right").astype(jnp.int32)
    table = labels.reshape(top, rows).T
    table = table[jax.random.permutation(jax.random.fold_in(own, 1), rows)]
    turn = jax.random.randint(jax.random.fold_in(own, 2), (rows, 1), 0, top)
    return jnp.take_along_axis(table, (jnp.arange(top)[None, :] + turn) % top, axis=1)


def load_shares(amount, total, limit, lean, full):
    loads = [(1 << 20) // math.isqrt(rank ** lean) + 1 for rank in range(1, amount + 1)]
    largest = limit if full else min(limit, max(-(-total // amount), total * loads[0] // sum(loads)))
    least = 1 if total - largest >= amount - 1 else 0
    holding, surplus = [largest] + [least] * (amount - 1), total - largest - least * (amount - 1)
    while surplus > 0:
        free = [i for i in range(1, amount) if holding[i] < largest] or [i for i in range(1, amount) if holding[i] < limit]
        mass, left = sum([loads[i] for i in free]), surplus
        for i in free:
            addition = min(limit - holding[i], max(1, left * loads[i] // mass), surplus)
            holding[i] = holding[i] + addition
            surplus = surplus - addition
    return np.array(holding)


def noise(own_key, extent, scale, bound, split=(), held_as=jnp.bfloat16):
    entries = scale * jax.random.normal(own_key, extent, jnp.float32)
    if split:
        entries = entries * block_scale(own_key, extent, split, -0.22, 0.18)
    return jnp.clip(entries, -bound, bound).astype(held_as)


def setup_inputs(seed: int = 0) -> dict:
    key_of = jax.random.split(jax.random.key(seed), 15)
    prompt_query = draw_prompt_query(jax.random.fold_in(key_of[14], 71), 0)
    prompt_keys = draw_prompt_keys(jax.random.fold_in(key_of[14], 71), 0)
    prompt_values = noise(key_of[2], (2, N_EXP, PROMPT_SLOTS, KEY_VALUE_HEADS * HEAD_SIZE), 4.0, 24.0, ((0, 2), (1, 2), (2, 8)))
    lengths = touch_ends(jax.random.randint(key_of[3], (2, N_EXP), PROMPT_SLOTS // 2 + 1, PROMPT_SLOTS + 1), jax.random.fold_in(key_of[3], 1), PROMPT_SLOTS // 2 + 1, PROMPT_SLOTS).astype(jnp.int32)
    decode_query = draw_decode_query(jax.random.fold_in(key_of[14], 71), 0)
    fresh_keys = noise(key_of[5], (2, N_EXP, DECODE_REQUESTS, KEY_VALUE_HEADS * HEAD_SIZE), 1.0, 6.0, ((0, 2), (1, 2)))
    fresh_values = noise(key_of[6], (2, N_EXP, DECODE_REQUESTS, KEY_VALUE_HEADS * HEAD_SIZE), 4.0, 24.0, ((0, 2), (1, 2)))
    x_dec = noise(key_of[7], (2, N_EXP, DECODE_REQUESTS, D), 0.1, 0.59765625, ((0, 2), (1, 2), (2, 8)))
    w_out = noise(key_of[8], (QUERY_HEADS * HEAD_SIZE, D), (QUERY_HEADS * HEAD_SIZE) ** -0.5, 0.125, ((0, 8),))
    norm_gain = jnp.clip(1.0 + 0.1 * jax.random.normal(key_of[9], (D,), jnp.float32), 0.5, 1.5).astype(jnp.bfloat16)
    w_gate_up = noise(key_of[10], (EXPERTS, D, 2 * FF), D ** -0.5, 0.125, ((0, 16),))
    w_down = noise(key_of[11], (EXPERTS, FF, D), FF ** -0.5, 0.21875, ((0, 16),))
    expert_ids_keys = jax.random.split(jax.random.fold_in(key_of[12], 1), 2 * N_EXP * DECODE_REQUESTS // ROWS_DEV)
    expert_ids_turns = jax.random.permutation(jax.random.fold_in(key_of[12], 3), 2 * N_EXP * DECODE_REQUESTS // ROWS_DEV)
    expert_ids = jax.vmap(lambda own, number: assign_block(jax.random.fold_in(key_of[12], 2), own, number, ROWS_DEV, EXPERTS, TOP, CAP, 1))(expert_ids_keys, expert_ids_turns).reshape((2, N_EXP, DECODE_REQUESTS, TOP))
    gate_weights = jnp.clip(jnp.exp(math.log(1.0) - 2.3025851 * jax.random.uniform(key_of[13], (2, N_EXP, DECODE_REQUESTS, TOP), jnp.float32) ** block_scale(key_of[13], (2, N_EXP, DECODE_REQUESTS, TOP), ((0, 2), (1, 2), (2, 8)), -0.2, 0.2)), 0.1, 1.0)
    return {"prompt_query": prompt_query, "prompt_keys": prompt_keys, "prompt_values": prompt_values, "lengths": lengths, "decode_query": decode_query, "fresh_keys": fresh_keys, "fresh_values": fresh_values, "x_dec": x_dec, "w_out": w_out, "norm_gain": norm_gain, "w_gate_up": w_gate_up, "w_down": w_down, "expert_ids": expert_ids, "gate_weights": gate_weights}


NEGATIVE_LIMIT = -1e+30
EPSILON = 1e-06

def reference(prompt_query, prompt_keys, prompt_values, lengths, decode_query, fresh_keys, fresh_values, x_dec, w_out, norm_gain, w_gate_up, w_down, expert_ids, gate_weights):
    group_width = QUERY_HEADS // KEY_VALUE_HEADS
    scaling = HEAD_SIZE ** (-0.5)
    block_size = math.gcd(PROMPT_SLOTS, 512)
    prompt_list = 2 * N_EXP

    def prefill_one_prompt(operands):
        query_vector, key_tensor, value_tensor, length = operands
        query_vector = query_vector.astype(jnp.float32).reshape(PROMPT_SLOTS, KEY_VALUE_HEADS, group_width, HEAD_SIZE)
        key_tensor = key_tensor.astype(jnp.float32).reshape(PROMPT_SLOTS, KEY_VALUE_HEADS, HEAD_SIZE)
        value_tensor = value_tensor.astype(jnp.float32).reshape(PROMPT_SLOTS, KEY_VALUE_HEADS, HEAD_SIZE)
        columns = jnp.arange(PROMPT_SLOTS, dtype=jnp.int32)

        def one_block(offset):
            rows_query = lax.dynamic_slice_in_dim(query_vector, offset, block_size, 0)
            row_pos = offset + jnp.arange(block_size, dtype=jnp.int32)
            scores = jnp.einsum('qhgd,khd->hgqk', rows_query, key_tensor) * scaling
            keep_mask = (columns[None, :] <= row_pos[:, None]) & (columns[None, :] < length)
            scores = jnp.where(keep_mask, scores, NEGATIVE_LIMIT)
            peak = scores.max(-1, keepdims=True)
            weights = jnp.where(keep_mask, jnp.exp(scores - peak), 0.0)
            totals = jnp.transpose(weights.sum(-1), (2, 0, 1))
            rounded = weights.astype(jnp.bfloat16).astype(jnp.float32)
            mixed = jnp.einsum('hgqk,khd->qhgd', rounded, value_tensor)
            mixed = mixed / jnp.where(totals > 0, totals, 1.0)[..., None]
            mixed = jnp.where((row_pos < length)[:, None, None, None], mixed, 0.0)
            return mixed.reshape(block_size, QUERY_HEADS * HEAD_SIZE).astype(jnp.bfloat16)
        offsets = jnp.arange(PROMPT_SLOTS // block_size, dtype=jnp.int32) * block_size
        return lax.map(one_block, offsets).reshape(PROMPT_SLOTS, QUERY_HEADS * HEAD_SIZE)
    prompt_attention = lax.map(prefill_one_prompt, (prompt_query.reshape(prompt_list, PROMPT_SLOTS, QUERY_HEADS * HEAD_SIZE), prompt_keys.reshape(prompt_list, PROMPT_SLOTS, KEY_VALUE_HEADS * HEAD_SIZE), prompt_values.reshape(prompt_list, PROMPT_SLOTS, KEY_VALUE_HEADS * HEAD_SIZE), lengths.reshape(prompt_list))).reshape(2, N_EXP, PROMPT_SLOTS, QUERY_HEADS * HEAD_SIZE)

    def decode_for_prompt(operands):
        query_vector, key_tensor, value_tensor, length, appended_keys, appended_values = operands
        query_vector = query_vector.astype(jnp.float32).reshape(DECODE_REQUESTS, KEY_VALUE_HEADS, group_width, HEAD_SIZE)
        key_tensor = key_tensor.astype(jnp.float32).reshape(PROMPT_SLOTS, KEY_VALUE_HEADS, HEAD_SIZE)
        value_tensor = value_tensor.astype(jnp.float32).reshape(PROMPT_SLOTS, KEY_VALUE_HEADS, HEAD_SIZE)
        appended_keys = appended_keys.astype(jnp.float32).reshape(DECODE_REQUESTS, KEY_VALUE_HEADS, HEAD_SIZE)
        appended_values = appended_values.astype(jnp.float32).reshape(DECODE_REQUESTS, KEY_VALUE_HEADS, HEAD_SIZE)
        columns = jnp.arange(PROMPT_SLOTS, dtype=jnp.int32)
        keep_mask = columns < length
        scores = jnp.einsum('shgd,khd->hgsk', query_vector, key_tensor) * scaling
        scores = jnp.where(keep_mask, scores, NEGATIVE_LIMIT)
        own_score = jnp.einsum('shgd,shd->hgs', query_vector, appended_keys) * scaling
        peak = jnp.maximum(scores.max(-1), own_score)
        weights = jnp.where(keep_mask, jnp.exp(scores - peak[..., None]), 0.0)
        own_weight = jnp.exp(own_score - peak)
        totals = weights.sum(-1) + own_weight
        mixed = jnp.einsum('hgsk,khd->hgsd', weights.astype(jnp.bfloat16).astype(jnp.float32), value_tensor)
        mixed = mixed + own_weight.astype(jnp.bfloat16).astype(jnp.float32)[..., None] * jnp.transpose(appended_values, (1, 0, 2))[:, None]
        mixed = mixed / totals[..., None]
        return jnp.transpose(mixed, (2, 0, 1, 3)).reshape(DECODE_REQUESTS, QUERY_HEADS * HEAD_SIZE).astype(jnp.bfloat16)
    decode_attention = lax.map(decode_for_prompt, (decode_query.reshape(prompt_list, DECODE_REQUESTS, QUERY_HEADS * HEAD_SIZE), prompt_keys[::-1].reshape(prompt_list, PROMPT_SLOTS, KEY_VALUE_HEADS * HEAD_SIZE), prompt_values[::-1].reshape(prompt_list, PROMPT_SLOTS, KEY_VALUE_HEADS * HEAD_SIZE), lengths[::-1].reshape(prompt_list), fresh_keys.reshape(prompt_list, DECODE_REQUESTS, KEY_VALUE_HEADS * HEAD_SIZE), fresh_values.reshape(prompt_list, DECODE_REQUESTS, KEY_VALUE_HEADS * HEAD_SIZE)))
    projected = jnp.dot(decode_attention.reshape(-1, QUERY_HEADS * HEAD_SIZE), w_out, preferred_element_type=jnp.float32).reshape(2, N_EXP, DECODE_REQUESTS, D)
    residual = x_dec.astype(jnp.float32) + projected
    normed = (residual * lax.rsqrt(lax.optimization_barrier(jnp.mean(residual * residual, -1, keepdims=True)) + EPSILON) * norm_gain.astype(jnp.float32)).astype(jnp.bfloat16)
    most_rows = N_CTX * N_EXP * CAP
    moe_parts = []
    for group_index in range(2):
        rows_flat = normed[group_index].reshape(-1, D)
        flat_ids = expert_ids[group_index].reshape(-1)
        flat_gates = gate_weights[group_index].reshape(-1)

        def expert_pass(carried, operands, rows_flat=rows_flat, flat_ids=flat_ids, flat_gates=flat_gates):
            gate_up, down, expert = operands
            chosen = flat_ids == expert
            slots = jnp.nonzero(chosen, size=most_rows, fill_value=0)[0].astype(jnp.int32)
            usable = jnp.arange(most_rows, dtype=jnp.int32) < jnp.sum(chosen.astype(jnp.int32))
            owners = slots // TOP
            gathered = rows_flat[owners]
            mixed = jnp.dot(gathered, gate_up, preferred_element_type=jnp.float32)
            hidden = (jax.nn.silu(mixed[:, :FF]) * mixed[:, FF:]).astype(jnp.bfloat16)
            output = jnp.dot(hidden, down, preferred_element_type=jnp.float32).astype(jnp.bfloat16).astype(jnp.float32)
            scaled = output * jnp.where(usable, flat_gates[slots], 0.0)[:, None]
            return (carried.at[owners].add(scaled), None)
        initial = jnp.zeros((N_EXP * DECODE_REQUESTS, D), jnp.float32)
        summed, unused_out = lax.scan(expert_pass, initial, (w_gate_up, w_down, jnp.arange(EXPERTS, dtype=jnp.int32)))
        moe_parts.append(summed)
    moe = jnp.stack(moe_parts).reshape(2, N_EXP, DECODE_REQUESTS, D)
    out_dec = (residual + moe).astype(jnp.bfloat16)
    return (prompt_attention, out_dec)
```

```python
import functools
import math

import jax
import jax.numpy as jnp
from jax import lax
from jax.experimental import pallas as pl
from jax.experimental.pallas import tpu as pltpu
from jax.sharding import PartitionSpec as P

HEAD_SIZE = 128
QUERY_HEADS = 16
KEY_VALUE_HEADS = 2

NEGATIVE_LIMIT = -1e30
EPSILON = 1e-06
MESH = pl.DeviceIdType.MESH
VMEM_LIMIT = 60 * 1024 * 1024


def ring_place(index, count):
    odd = index % 2
    return (1 - odd) * (index // 2) + odd * (count - 1 - index // 2)


def ring_index(place, count):
    half = place // ((count + 1) // 2)
    return (1 - half) * 2 * place + half * (2 * (count - 1 - place) + 1)


def ring_gather_kernel(n, n_exp, split, *refs):
    n_in = 1 if split else 2
    ins, outs = refs[:n_in], refs[n_in : 2 * n_in]
    send_sem, recv_sem, peer_send, peer_recv, own_sem = refs[2 * n_in :]
    me = lax.axis_index("ctx")
    mine = lax.axis_index("exp") if n_exp > 1 else 0
    place = ring_place(me, n)
    hops = n // 2

    if split:
        width = ins[0].shape[1] // 2
        source = lambda part: ins[0].at[:, pl.ds(part * width, width)]
        slot = lambda part, index: outs[0].at[index, mine, :, pl.ds(part * width, width)]
    else:
        source = lambda part: ins[part]
        slot = lambda part, index: outs[part].at[index, mine]

    def neighbour(step):
        return ring_index((place + step + n) % n, n)

    barrier = pltpu.get_barrier_semaphore()
    for step in (-1, 1):
        pl.semaphore_signal(barrier, inc=1, device_id={"ctx": neighbour(step)}, device_id_type=MESH)
    for shift in range(1, n_exp):
        pl.semaphore_signal(
            barrier, inc=1, device_id={"exp": (mine + shift) % n_exp}, device_id_type=MESH
        )
    pl.semaphore_wait(barrier, 2 + n_exp - 1)

    started = {}
    peers = []

    def pass_on(part, message, src, index):
        for shift in range(1, n_exp):
            copy = pltpu.make_async_remote_copy(
                src_ref=src,
                dst_ref=slot(part, index),
                send_sem=peer_send.at[part, message, shift - 1],
                recv_sem=peer_recv.at[part, message, shift - 1],
                device_id={"exp": (mine + shift) % n_exp},
                device_id_type=MESH,
            )
            copy.start()
            peers.append(copy)

    flows = [(0, 1, hops), (1, -1, hops), (1, 1, n - 1 - hops), (0, -1, n - 1 - hops)]
    for hop in range(1, hops + 2):
        for part, step, most in flows:
            way = (step + 1) // 2
            index = ring_index((place - step * (hop - 1) + n * hop) % n, n)
            if hop > 1 and hop - 1 <= most:
                started[part, way, hop - 1].wait_recv()
            if hop <= most:
                copy = pltpu.make_async_remote_copy(
                    src_ref=source(part) if hop == 1 else slot(part, index),
                    dst_ref=slot(part, index),
                    send_sem=send_sem.at[part, way, hop - 1],
                    recv_sem=recv_sem.at[part, way, hop - 1],
                    device_id={"ctx": neighbour(step)},
                    device_id_type=MESH,
                )
                copy.start()
                started[part, way, hop] = copy
            if hop > 1 and hop - 1 <= most:
                pass_on(part, 1 + way * hops + hop - 2, slot(part, index), index)
        if hop == 1:
            own = []
            for part in range(2):
                copy = pltpu.make_async_copy(source(part), slot(part, me), own_sem.at[part])
                copy.start()
                own.append(copy)
                pass_on(part, 0, source(part), me)
    for copy in own:
        copy.wait()
    for copy in started.values():
        copy.wait_send()
    for copy in peers:
        copy.wait()


def ring_gather(arrays, n, n_exp, collective_id):
    split = len(arrays) == 1
    hops = n // 2
    outs = [jax.ShapeDtypeStruct((n, n_exp) + a.shape, a.dtype) for a in arrays]
    return pl.pallas_call(
        functools.partial(ring_gather_kernel, n, n_exp, split),
        out_shape=outs,
        in_specs=[pl.BlockSpec(memory_space=pltpu.VMEM)] * len(arrays),
        out_specs=[pl.BlockSpec(memory_space=pltpu.VMEM)] * len(arrays),
        scratch_shapes=[
            pltpu.SemaphoreType.DMA((2, 2, hops)),
            pltpu.SemaphoreType.DMA((2, 2, hops)),
            pltpu.SemaphoreType.DMA((2, 1 + 2 * hops, max(1, n_exp - 1))),
            pltpu.SemaphoreType.DMA((2, 1 + 2 * hops, max(1, n_exp - 1))),
            pltpu.SemaphoreType.DMA((2,)),
        ],
        compiler_params=pltpu.CompilerParams(collective_id=collective_id, has_side_effects=True),
        name="ring_gather",
    )(*arrays)


def attend_kernel(heads, causal, tile, info, *refs):
    if causal:
        q_ref, k_ref, v_ref, out_ref = refs
    else:
        q_ref, k_ref, v_ref, fk_ref, fv_ref, out_ref = refs
    rows = q_ref.shape[0]
    factor = HEAD_SIZE ** (-0.5) * math.log2(math.e)
    length, base = info[0], info[1]
    if causal:
        free = jnp.minimum(length, base) // tile
        limit = jnp.where(base < length, jnp.minimum(length, base + rows), 0)
    else:
        free = length // tile
        limit = length
    last = (limit + tile - 1) // tile
    free = jnp.minimum(free, last)
    queries = [q_ref[:, h * HEAD_SIZE : (h + 1) * HEAD_SIZE] for h in range(heads)]
    carry = []
    for h in range(heads):
        if causal:
            carry += [
                jnp.full((rows, 1), NEGATIVE_LIMIT, jnp.float32),
                jnp.zeros((rows, 1), jnp.float32),
                jnp.zeros((rows, HEAD_SIZE), jnp.float32),
            ]
        else:
            own = jnp.sum(
                queries[h].astype(jnp.float32) * fk_ref[...].astype(jnp.float32), -1, keepdims=True
            )
            carry += [
                own * factor,
                jnp.ones((rows, 1), jnp.float32),
                fv_ref[...].astype(jnp.float32),
            ]

    def step(masked, j, carry):
        start = pl.multiple_of(j * tile, tile)
        keys = k_ref[pl.ds(start, tile), :]
        values = v_ref[pl.ds(start, tile), :]
        if masked:
            column = start + lax.broadcasted_iota(jnp.int32, (rows, tile), 1)
            keep = column < length
            if causal:
                row = base + lax.broadcasted_iota(jnp.int32, (rows, tile), 0)
                keep = keep & (column <= row)
        result = []
        for h in range(heads):
            peak, total, weighted = carry[3 * h : 3 * h + 3]
            scores = lax.dot_general(
                queries[h], keys, (((1,), (1,)), ((), ())), preferred_element_type=jnp.float32
            )
            scores = scores * factor
            if masked:
                scores = jnp.where(keep, scores, NEGATIVE_LIMIT)
            new_peak = jnp.maximum(peak, jnp.max(scores, -1, keepdims=True))
            rescale = jnp.exp2(peak - new_peak)
            weights = jnp.exp2(scores - new_peak)
            if masked:
                weights = jnp.where(keep, weights, 0.0)
            total = rescale * total + jnp.sum(weights, -1, keepdims=True)
            weighted = rescale * weighted + jnp.dot(
                weights.astype(jnp.bfloat16), values, preferred_element_type=jnp.float32
            )
            result += [new_peak, total, weighted]
        return tuple(result)

    carry = lax.fori_loop(0, free, functools.partial(step, False), tuple(carry))
    carry = lax.fori_loop(free, last, functools.partial(step, True), carry)
    for h in range(heads):
        peak, total, weighted = carry[3 * h : 3 * h + 3]
        mixed = weighted / jnp.where(total > 0, total, 1.0)
        if causal:
            row = base + lax.broadcasted_iota(jnp.int32, (rows, HEAD_SIZE), 0)
            mixed = jnp.where(row < length, mixed, 0.0)
        out_ref[:, h * HEAD_SIZE : (h + 1) * HEAD_SIZE] = mixed.astype(jnp.bfloat16)


def attend(info, queries, keys, values, fresh=None):
    causal = fresh is None
    rows, width = queries.shape
    count = width // HEAD_SIZE
    group_width = QUERY_HEADS // KEY_VALUE_HEADS
    heads = math.gcd(count, 4)
    prompt_len = keys.shape[0]
    tile = math.gcd(prompt_len, 512)
    if causal:
        head_of = lambda i, info: (0, i * heads // group_width)
    else:
        head_of = lambda i, info: (0, info[2])
    in_specs = [
        pl.BlockSpec((rows, heads * HEAD_SIZE), lambda i, info: (0, i)),
        pl.BlockSpec((prompt_len, HEAD_SIZE), head_of),
        pl.BlockSpec((prompt_len, HEAD_SIZE), head_of),
    ]
    operands = [queries, keys, values]
    if not causal:
        in_specs += [pl.BlockSpec((rows, HEAD_SIZE), lambda i, info: (0, 0))] * 2
        operands += list(fresh)
    return pl.pallas_call(
        functools.partial(attend_kernel, heads, causal, tile),
        out_shape=jax.ShapeDtypeStruct((rows, width), jnp.bfloat16),
        grid_spec=pltpu.PrefetchScalarGridSpec(
            num_scalar_prefetch=1,
            grid=(count // heads,),
            in_specs=in_specs,
            out_specs=pl.BlockSpec((rows, heads * HEAD_SIZE), lambda i, info: (0, i)),
        ),
        compiler_params=pltpu.CompilerParams(dimension_semantics=("arbitrary",)),
        cost_estimate=pl.CostEstimate(
            flops=4 * rows * width * prompt_len,
            bytes_accessed=4 * rows * width + 4 * prompt_len * HEAD_SIZE,
            transcendentals=rows * count * prompt_len,
        ),
        name="prefill" if causal else "decode",
    )(info, *operands)


def body(
    prompt_query,
    prompt_keys,
    prompt_values,
    lengths,
    decode_query,
    fresh_keys,
    fresh_values,
    x_dec,
    w_out,
    norm_gain,
    w_gate_up,
    w_down,
    expert_ids,
    gate_weights,
):
    group_width = QUERY_HEADS // KEY_VALUE_HEADS
    my_group = lax.axis_index("group")
    ctx_index = lax.axis_index("ctx")
    n_ctx = lax.axis_size("ctx")
    n_exp = lax.axis_size("exp")
    length_mine = lax.dynamic_index_in_dim(lengths[:, 0], my_group, keepdims=False)
    token_rows = prompt_query.shape[2]
    prompt_len = token_rows * n_ctx
    local_heads = decode_query.shape[3] // HEAD_SIZE
    samples = decode_query.shape[2]
    kv_head = ctx_index * local_heads // group_width
    info = jnp.stack([length_mine, ctx_index * token_rows, kv_head]).astype(jnp.int32)
    partner = [(0, 1), (1, 0)]

    own_keys = lax.dynamic_slice_in_dim(fresh_keys[0, 0], kv_head * HEAD_SIZE, HEAD_SIZE, 1)
    own_values = lax.dynamic_slice_in_dim(fresh_values[0, 0], kv_head * HEAD_SIZE, HEAD_SIZE, 1)
    far_query, far_keys, far_values = lax.ppermute(
        (decode_query[0, 0], own_keys, own_values), "group", partner
    )

    keys, values = ring_gather((prompt_keys[0, 0], prompt_values[0, 0]), n_ctx, 1, 0)
    keys = keys.reshape(prompt_len, keys.shape[-1])
    values = values.reshape(prompt_len, values.shape[-1])

    far_attn = attend(info, far_query, keys, values, (far_keys, far_values))
    dec_attn = lax.ppermute(far_attn, "group", partner)
    row_count = x_dec.shape[2]
    shares = jnp.dot(dec_attn, w_out, preferred_element_type=jnp.float32).astype(jnp.bfloat16)
    shares = shares.reshape(n_ctx, row_count, shares.shape[1])
    shares = lax.all_to_all(shares, "ctx", split_axis=0, concat_axis=0, tiled=True)

    prompt_attn = attend(info, prompt_query[0, 0], keys, values)
    prompt_attention = prompt_attn.reshape(prompt_query.shape)

    projected = jnp.sum(shares.astype(jnp.float32), 0)
    residual = x_dec[0, 0].astype(jnp.float32) + projected
    normed = (
        residual
        * lax.rsqrt(jnp.mean(residual * residual, -1, keepdims=True) + EPSILON)
        * norm_gain.astype(jnp.float32)
    ).astype(jnp.bfloat16)
    model_width = normed.shape[1]
    top_count = expert_ids.shape[3]
    experts_all = w_gate_up.shape[0] * n_ctx * n_exp
    capacity = min(row_count, max(2, 2 * row_count * top_count // experts_all))
    every_row = capacity == row_count
    ids = expert_ids[0, 0]
    chosen = ids[:, :, None] == lax.iota(jnp.int32, experts_all)[None, None, :]
    if every_row:
        (arrived,) = ring_gather((normed,), n_ctx, n_exp, 1)
    else:
        one_hot = chosen.reshape(-1, experts_all).astype(jnp.int32)
        earlier = jnp.cumsum(one_hot, 0) - one_hot
        target = ids.reshape(-1) * capacity + jnp.sum(earlier * one_hot, 1)
        placing = (
            lax.iota(jnp.int32, experts_all * capacity)[:, None, None]
            == target.reshape(row_count, top_count)[None]
        ).any(-1)
        buffer = jnp.dot(
            placing.astype(jnp.bfloat16), normed, preferred_element_type=jnp.float32
        ).astype(jnp.bfloat16)
        buffer = buffer.reshape(experts_all, capacity, model_width)
        arrived = lax.all_to_all(buffer, ("ctx", "exp"), split_axis=0, concat_axis=0, tiled=True)
    flat_rows = arrived.reshape(-1, model_width)
    mixed = jnp.dot(flat_rows, w_gate_up[0], preferred_element_type=jnp.float32)
    hidden_units = mixed.shape[1] // 2
    hidden = (jax.nn.silu(mixed[:, :hidden_units]) * mixed[:, hidden_units:]).astype(jnp.bfloat16)
    produced = jnp.dot(hidden, w_down[0], preferred_element_type=jnp.float32).astype(jnp.bfloat16)
    outputs = produced.reshape(experts_all, capacity, model_width)
    returned = lax.all_to_all(outputs, ("ctx", "exp"), split_axis=0, concat_axis=0, tiled=True)
    gate_values = gate_weights[0, 0]
    if every_row:
        gates = jnp.sum(jnp.where(chosen, gate_values[:, :, None], 0.0), 1)
        moe = jnp.sum(returned.astype(jnp.float32) * gates.T[:, :, None], 0)
    else:
        picked = returned.reshape(experts_all * capacity, model_width)[target]
        moe = jnp.sum(
            picked.reshape(row_count, top_count, model_width).astype(jnp.float32)
            * gate_values[..., None],
            1,
        )
    out_dec = (residual + moe).astype(jnp.bfloat16).reshape(1, 1, row_count, model_width)
    return (prompt_attention, out_dec)


def solution(mesh):
    in_specs = (
        P("group", "exp", "ctx", None),
        P("group", "exp", "ctx", None),
        P("group", "exp", "ctx", None),
        P(None, "exp"),
        P("group", "exp", None, "ctx"),
        P("group", "exp", None, None),
        P("group", "exp", None, None),
        P("group", "exp", "ctx", None),
        P("ctx", None),
        P(),
        P(("ctx", "exp"), None, None),
        P(("ctx", "exp"), None, None),
        P("group", "exp", "ctx", None),
        P("group", "exp", "ctx", None),
    )
    out_specs = (P("group", "exp", "ctx", None), P("group", "exp", "ctx", None))
    return jax.shard_map(body, mesh=mesh, in_specs=in_specs, out_specs=out_specs, check_vma=False)
```

```python
import functools
import math

import jax
import jax.numpy as jnp
from jax import lax
from jax.experimental import pallas as pl
from jax.experimental.pallas import tpu as pltpu
from jax.sharding import PartitionSpec as P

HEAD_SIZE = 128
QUERY_HEADS = 16
KEY_VALUE_HEADS = 2

NEGATIVE_LIMIT = -1e30
EPSILON = 1e-06
MESH = pl.DeviceIdType.MESH
VMEM_LIMIT = 60 * 1024 * 1024


def ring_place(index, count):
    odd = index % 2
    return (1 - odd) * (index // 2) + odd * (count - 1 - index // 2)


def ring_index(place, count):
    half = place // ((count + 1) // 2)
    return (1 - half) * 2 * place + half * (2 * (count - 1 - place) + 1)


def ring_gather_kernel(n, n_exp, split, *refs):
    n_in = 1 if split else 2
    ins, outs = refs[:n_in], refs[n_in : 2 * n_in]
    send_sem, recv_sem, peer_send, peer_recv, own_sem = refs[2 * n_in :]
    me = lax.axis_index("ctx")
    mine = lax.axis_index("exp") if n_exp > 1 else 0
    place = ring_place(me, n)
    hops = n // 2

    if split:
        width = ins[0].shape[1] // 2
        source = lambda part: ins[0].at[:, pl.ds(part * width, width)]
        slot = lambda part, index: outs[0].at[index, mine, :, pl.ds(part * width, width)]
    else:
        source = lambda part: ins[part]
        slot = lambda part, index: outs[part].at[index, mine]

    def neighbour(step):
        return ring_index((place + step + n) % n, n)

    barrier = pltpu.get_barrier_semaphore()
    for step in (-1, 1):
        pl.semaphore_signal(barrier, inc=1, device_id={"ctx": neighbour(step)}, device_id_type=MESH)
    for shift in range(1, n_exp):
        pl.semaphore_signal(
            barrier, inc=1, device_id={"exp": (mine + shift) % n_exp}, device_id_type=MESH
        )
    pl.semaphore_wait(barrier, 2 + n_exp - 1)

    started = {}
    peers = []

    def pass_on(part, message, src, index):
        for shift in range(1, n_exp):
            copy = pltpu.make_async_remote_copy(
                src_ref=src,
                dst_ref=slot(part, index),
                send_sem=peer_send.at[part, message, shift - 1],
                recv_sem=peer_recv.at[part, message, shift - 1],
                device_id={"exp": (mine + shift) % n_exp},
                device_id_type=MESH,
            )
            copy.start()
            peers.append(copy)

    flows = [(0, 1, hops), (1, -1, hops), (1, 1, n - 1 - hops), (0, -1, n - 1 - hops)]
    for hop in range(1, hops + 2):
        for part, step, most in flows:
            way = (step + 1) // 2
            index = ring_index((place - step * (hop - 1) + n * hop) % n, n)
            if hop > 1 and hop - 1 <= most:
                started[part, way, hop - 1].wait_recv()
            if hop <= most:
                copy = pltpu.make_async_remote_copy(
                    src_ref=source(part) if hop == 1 else slot(part, index),
                    dst_ref=slot(part, index),
                    send_sem=send_sem.at[part, way, hop - 1],
                    recv_sem=recv_sem.at[part, way, hop - 1],
                    device_id={"ctx": neighbour(step)},
                    device_id_type=MESH,
                )
                copy.start()
                started[part, way, hop] = copy
            if hop > 1 and hop - 1 <= most:
                pass_on(part, 1 + way * hops + hop - 2, slot(part, index), index)
        if hop == 1:
            own = []
            for part in range(2):
                copy = pltpu.make_async_copy(source(part), slot(part, me), own_sem.at[part])
                copy.start()
                own.append(copy)
                pass_on(part, 0, source(part), me)
    for copy in own:
        copy.wait()
    for copy in started.values():
        copy.wait_send()
    for copy in peers:
        copy.wait()


def ring_gather(arrays, n, n_exp, collective_id):
    split = len(arrays) == 1
    hops = n // 2
    outs = [jax.ShapeDtypeStruct((n, n_exp) + a.shape, a.dtype) for a in arrays]
    return pl.pallas_call(
        functools.partial(ring_gather_kernel, n, n_exp, split),
        out_shape=outs,
        in_specs=[pl.BlockSpec(memory_space=pltpu.VMEM)] * len(arrays),
        out_specs=[pl.BlockSpec(memory_space=pltpu.VMEM)] * len(arrays),
        scratch_shapes=[
            pltpu.SemaphoreType.DMA((2, 2, hops)),
            pltpu.SemaphoreType.DMA((2, 2, hops)),
            pltpu.SemaphoreType.DMA((2, 1 + 2 * hops, max(1, n_exp - 1))),
            pltpu.SemaphoreType.DMA((2, 1 + 2 * hops, max(1, n_exp - 1))),
            pltpu.SemaphoreType.DMA((2,)),
        ],
        compiler_params=pltpu.CompilerParams(collective_id=collective_id, has_side_effects=True),
        name="ring_gather",
    )(*arrays)


def ring_decode_kernel(n, local_heads, *refs):
    (k_ref, v_ref, q_ref, fk_ref, fv_ref, lengths) = refs[:6]
    k_out, v_out, attn_out = refs[6:9]
    (far_q, far_k, far_v, near_attn, send_sem, recv_sem, swap_send, swap_recv, own_sem) = refs[9:]
    group = lax.axis_index("group")
    me = lax.axis_index("ctx")
    place = ring_place(me, n)
    hops = n // 2
    group_width = QUERY_HEADS // KEY_VALUE_HEADS
    column = pl.multiple_of(me * local_heads // group_width * HEAD_SIZE, HEAD_SIZE)
    head_columns = pl.ds(column, HEAD_SIZE)
    ins, outs = (k_ref, v_ref), (k_out, v_out)
    rows = k_ref.shape[0]
    samples = q_ref.shape[0]
    factor = HEAD_SIZE ** (-0.5) * math.log2(math.e)

    def neighbour(step):
        return ring_index((place + step + n) % n, n)

    barrier = pltpu.get_barrier_semaphore()
    for step in (-1, 1):
        pl.semaphore_signal(barrier, inc=1, device_id={"ctx": neighbour(step)}, device_id_type=MESH)
    pl.semaphore_signal(barrier, inc=1, device_id={"group": 1 - group}, device_id_type=MESH)
    pl.semaphore_wait(barrier, 3)

    def swap(number, src, dst):
        return pltpu.make_async_remote_copy(
            src_ref=src,
            dst_ref=dst,
            send_sem=swap_send.at[number],
            recv_sem=swap_recv.at[number],
            device_id={"group": 1 - group},
            device_id_type=MESH,
        )

    swaps = [
        swap(0, q_ref, far_q),
        swap(1, fk_ref.at[:, head_columns], far_k),
        swap(2, fv_ref.at[:, head_columns], far_v),
    ]
    flows = [(0, 1, hops), (1, -1, hops), (1, 1, n - 1 - hops), (0, -1, n - 1 - hops)]
    started = {}

    def send(hop):
        for part, step, most in flows:
            way = (step + 1) // 2
            if 1 < hop <= most + 1:
                started[part, way, hop - 1].wait_recv()
            if hop <= most:
                index = ring_index((place - step * (hop - 1) + n * hop) % n, n)
                copy = pltpu.make_async_remote_copy(
                    src_ref=ins[part] if hop == 1 else outs[part].at[index],
                    dst_ref=outs[part].at[index],
                    send_sem=send_sem.at[part, way, hop - 1],
                    recv_sem=recv_sem.at[part, way, hop - 1],
                    device_id={"ctx": neighbour(step)},
                    device_id_type=MESH,
                )
                copy.start()
                started[part, way, hop] = copy

    send(1)
    for copy in swaps:
        copy.start()
    own = [
        pltpu.make_async_copy(ins[part], outs[part].at[me], own_sem.at[part]) for part in range(2)
    ]
    for copy in own:
        copy.start()
    length = lengths[group, 0]
    for copy in swaps:
        copy.wait()
    queries = jnp.concatenate(
        [far_q[:, h * HEAD_SIZE : (h + 1) * HEAD_SIZE] for h in range(local_heads)], 0
    )
    fresh_k = jnp.concatenate([far_k[...].astype(jnp.float32)] * local_heads, 0)
    fresh_v = jnp.concatenate([far_v[...].astype(jnp.float32)] * local_heads, 0)
    peak = jnp.sum(queries.astype(jnp.float32) * fresh_k, -1, keepdims=True) * factor
    state = (peak, jnp.ones_like(peak), fresh_v)

    def advance(state, keys, values, index):
        peak, total, weighted = state
        scores = (
            lax.dot_general(
                queries, keys, (((1,), (1,)), ((), ())), preferred_element_type=jnp.float32
            )
            * factor
        )
        keep = index * rows + lax.broadcasted_iota(jnp.int32, scores.shape, 1) < length
        scores = jnp.where(keep, scores, NEGATIVE_LIMIT)
        new_peak = jnp.maximum(peak, jnp.max(scores, -1, keepdims=True))
        rescale = jnp.exp2(peak - new_peak)
        weights = jnp.where(keep, jnp.exp2(scores - new_peak), 0.0)
        total = rescale * total + jnp.sum(weights, -1, keepdims=True)
        weighted = rescale * weighted + jnp.dot(
            weights.astype(jnp.bfloat16), values, preferred_element_type=jnp.float32
        )
        return new_peak, total, weighted

    state = advance(state, k_ref[:, head_columns], v_ref[:, head_columns], me)
    for hop in range(2, hops + 2):
        send(hop)
        steps = (1, -1) if hop - 1 <= n - 1 - hops else (1,)
        for step in steps:
            index = ring_index((place - step * (hop - 1) + n * hop) % n, n)
            state = advance(
                state, k_out[index, :, head_columns], v_out[index, :, head_columns], index
            )
    peak, total, weighted = state
    mixed = (weighted / total).astype(jnp.bfloat16)
    for h in range(local_heads):
        near_attn[:, h * HEAD_SIZE : (h + 1) * HEAD_SIZE] = mixed[h * samples : (h + 1) * samples]
    back = swap(3, near_attn, attn_out)
    back.start()
    for copy in own:
        copy.wait()
    for copy in started.values():
        copy.wait_send()
    back.wait()


def ring_decode(keys, values, query, fresh_keys, fresh_values, lengths, n):
    rows, samples = keys.shape[0], query.shape[0]
    hops = n // 2
    gathered = jax.ShapeDtypeStruct((n,) + keys.shape, keys.dtype)
    vmem = pl.BlockSpec(memory_space=pltpu.VMEM)
    return pl.pallas_call(
        functools.partial(ring_decode_kernel, n, query.shape[1] // HEAD_SIZE),
        out_shape=[gathered, gathered, jax.ShapeDtypeStruct(query.shape, jnp.bfloat16)],
        in_specs=[vmem] * 5 + [pl.BlockSpec(memory_space=pltpu.SMEM)],
        out_specs=[vmem] * 3,
        scratch_shapes=[
            pltpu.VMEM(query.shape, jnp.bfloat16),
            pltpu.VMEM((samples, HEAD_SIZE), jnp.bfloat16),
            pltpu.VMEM((samples, HEAD_SIZE), jnp.bfloat16),
            pltpu.VMEM(query.shape, jnp.bfloat16),
            pltpu.SemaphoreType.DMA((2, 2, hops)),
            pltpu.SemaphoreType.DMA((2, 2, hops)),
            pltpu.SemaphoreType.DMA((4,)),
            pltpu.SemaphoreType.DMA((4,)),
            pltpu.SemaphoreType.DMA((2,)),
        ],
        compiler_params=pltpu.CompilerParams(collective_id=0, has_side_effects=True),
        name="ring_decode",
    )(keys, values, query, fresh_keys, fresh_values, lengths)


def prefill_kernel(heads, tile, lengths, q_ref, k_ref, v_ref, out_ref):
    rows = q_ref.shape[0]
    factor = HEAD_SIZE ** (-0.5) * math.log2(math.e)
    length = lengths[lax.axis_index("group"), 0]
    base = lax.axis_index("ctx") * rows
    limit = jnp.where(base < length, jnp.minimum(length, base + rows), 0)
    last = (limit + tile - 1) // tile
    free = jnp.minimum(jnp.minimum(length, base) // tile, last)
    queries = [q_ref[:, h * HEAD_SIZE : (h + 1) * HEAD_SIZE] for h in range(heads)]
    carry = [
        jnp.full((rows, 1), NEGATIVE_LIMIT, jnp.float32),
        jnp.zeros((rows, 1), jnp.float32),
        jnp.zeros((rows, HEAD_SIZE), jnp.float32),
    ] * heads

    def step(masked, j, carry):
        start = pl.multiple_of(j * tile, tile)
        keys = k_ref[pl.ds(start, tile), :]
        values = v_ref[pl.ds(start, tile), :]
        if masked:
            column = start + lax.broadcasted_iota(jnp.int32, (rows, tile), 1)
            row = base + lax.broadcasted_iota(jnp.int32, (rows, tile), 0)
            keep = (column < length) & (column <= row)
        result = []
        for h in range(heads):
            peak, total, weighted = carry[3 * h : 3 * h + 3]
            scores = (
                lax.dot_general(
                    queries[h], keys, (((1,), (1,)), ((), ())), preferred_element_type=jnp.float32
                )
                * factor
            )
            if masked:
                scores = jnp.where(keep, scores, NEGATIVE_LIMIT)
            new_peak = jnp.maximum(peak, jnp.max(scores, -1, keepdims=True))
            rescale = jnp.exp2(peak - new_peak)
            weights = jnp.exp2(scores - new_peak)
            if masked:
                weights = jnp.where(keep, weights, 0.0)
            total = rescale * total + jnp.sum(weights, -1, keepdims=True)
            weighted = rescale * weighted + jnp.dot(
                weights.astype(jnp.bfloat16), values, preferred_element_type=jnp.float32
            )
            result += [new_peak, total, weighted]
        return tuple(result)

    carry = lax.fori_loop(0, free, functools.partial(step, False), tuple(carry))
    carry = lax.fori_loop(free, last, functools.partial(step, True), carry)
    row = base + lax.broadcasted_iota(jnp.int32, (rows, HEAD_SIZE), 0)
    for h in range(heads):
        peak, total, weighted = carry[3 * h : 3 * h + 3]
        mixed = weighted / jnp.where(total > 0, total, 1.0)
        mixed = jnp.where(row < length, mixed, 0.0)
        out_ref[:, h * HEAD_SIZE : (h + 1) * HEAD_SIZE] = mixed.astype(jnp.bfloat16)


def prefill(lengths, queries, keys, values):
    rows, width = queries.shape
    count = width // HEAD_SIZE
    group_width = QUERY_HEADS // KEY_VALUE_HEADS
    heads = math.gcd(group_width, 4)
    prompt_len = keys.shape[0]
    kv_spec = pl.BlockSpec((prompt_len, HEAD_SIZE), lambda i, info: (0, i * heads // group_width))
    q_spec = pl.BlockSpec((rows, heads * HEAD_SIZE), lambda i, info: (0, i))
    return pl.pallas_call(
        functools.partial(prefill_kernel, heads, math.gcd(prompt_len, 512)),
        out_shape=jax.ShapeDtypeStruct((rows, width), jnp.bfloat16),
        grid_spec=pltpu.PrefetchScalarGridSpec(
            num_scalar_prefetch=1,
            grid=(count // heads,),
            in_specs=[q_spec, kv_spec, kv_spec],
            out_specs=q_spec,
        ),
        compiler_params=pltpu.CompilerParams(dimension_semantics=("arbitrary",)),
        cost_estimate=pl.CostEstimate(
            flops=4 * rows * width * prompt_len,
            bytes_accessed=4 * rows * width + 4 * prompt_len * keys.shape[1],
            transcendentals=rows * count * prompt_len,
        ),
        name="prefill",
    )(lengths, queries, keys, values)


def body(
    prompt_query,
    prompt_keys,
    prompt_values,
    lengths,
    decode_query,
    fresh_keys,
    fresh_values,
    x_dec,
    w_out,
    norm_gain,
    w_gate_up,
    w_down,
    expert_ids,
    gate_weights,
):
    n_ctx = lax.axis_size("ctx")
    n_exp = lax.axis_size("exp")
    prompt_len = prompt_query.shape[2] * n_ctx
    keys, values, dec_attn = ring_decode(
        prompt_keys[0, 0],
        prompt_values[0, 0],
        decode_query[0, 0],
        fresh_keys[0, 0],
        fresh_values[0, 0],
        lengths,
        n_ctx,
    )
    keys = keys.reshape(prompt_len, keys.shape[-1])
    values = values.reshape(prompt_len, values.shape[-1])
    row_count = x_dec.shape[2]
    shares = jnp.dot(dec_attn, w_out, preferred_element_type=jnp.float32).astype(jnp.bfloat16)
    shares = shares.reshape(n_ctx, row_count, shares.shape[1])
    shares = lax.all_to_all(shares, "ctx", split_axis=0, concat_axis=0, tiled=True)

    prompt_attn = prefill(lengths, prompt_query[0, 0], keys, values)
    prompt_attention = prompt_attn.reshape(prompt_query.shape)

    projected = jnp.sum(shares.astype(jnp.float32), 0)
    residual = x_dec[0, 0].astype(jnp.float32) + projected
    normed = (
        residual
        * lax.rsqrt(jnp.mean(residual * residual, -1, keepdims=True) + EPSILON)
        * norm_gain.astype(jnp.float32)
    ).astype(jnp.bfloat16)
    model_width = normed.shape[1]
    top_count = expert_ids.shape[3]
    experts_all = w_gate_up.shape[0] * n_ctx * n_exp
    capacity = min(row_count, max(2, 2 * row_count * top_count // experts_all))
    every_row = capacity == row_count
    ids = expert_ids[0, 0]
    chosen = ids[:, :, None] == lax.iota(jnp.int32, experts_all)[None, None, :]
    if every_row:
        (arrived,) = ring_gather((normed,), n_ctx, n_exp, 1)
    else:
        one_hot = chosen.reshape(-1, experts_all).astype(jnp.int32)
        earlier = jnp.cumsum(one_hot, 0) - one_hot
        target = ids.reshape(-1) * capacity + jnp.sum(earlier * one_hot, 1)
        placing = (
            lax.iota(jnp.int32, experts_all * capacity)[:, None, None]
            == target.reshape(row_count, top_count)[None]
        ).any(-1)
        buffer = jnp.dot(
            placing.astype(jnp.bfloat16), normed, preferred_element_type=jnp.float32
        ).astype(jnp.bfloat16)
        buffer = buffer.reshape(experts_all, capacity, model_width)
        arrived = lax.all_to_all(buffer, ("ctx", "exp"), split_axis=0, concat_axis=0, tiled=True)
    flat_rows = arrived.reshape(-1, model_width)
    mixed = jnp.dot(flat_rows, w_gate_up[0], preferred_element_type=jnp.float32)
    hidden_units = mixed.shape[1] // 2
    hidden = (jax.nn.silu(mixed[:, :hidden_units]) * mixed[:, hidden_units:]).astype(jnp.bfloat16)
    produced = jnp.dot(hidden, w_down[0], preferred_element_type=jnp.float32).astype(jnp.bfloat16)
    outputs = produced.reshape(experts_all, capacity, model_width)
    returned = lax.all_to_all(outputs, ("ctx", "exp"), split_axis=0, concat_axis=0, tiled=True)
    gate_values = gate_weights[0, 0]
    if every_row:
        gates = jnp.sum(jnp.where(chosen, gate_values[:, :, None], 0.0), 1)
        moe = jnp.sum(returned.astype(jnp.float32) * gates.T[:, :, None], 0)
    else:
        picked = returned.reshape(experts_all * capacity, model_width)[target]
        moe = jnp.sum(
            picked.reshape(row_count, top_count, model_width).astype(jnp.float32)
            * gate_values[..., None],
            1,
        )
    out_dec = (residual + moe).astype(jnp.bfloat16).reshape(1, 1, row_count, model_width)
    return (prompt_attention, out_dec)


def solution(mesh):
    in_specs = (
        P("group", "exp", "ctx", None),
        P("group", "exp", "ctx", None),
        P("group", "exp", "ctx", None),
        P(None, "exp"),
        P("group", "exp", None, "ctx"),
        P("group", "exp", None, None),
        P("group", "exp", None, None),
        P("group", "exp", "ctx", None),
        P("ctx", None),
        P(),
        P(("ctx", "exp"), None, None),
        P(("ctx", "exp"), None, None),
        P("group", "exp", "ctx", None),
        P("group", "exp", "ctx", None),
    )
    out_specs = (P("group", "exp", "ctx", None), P("group", "exp", "ctx", None))
    return jax.shard_map(body, mesh=mesh, in_specs=in_specs, out_specs=out_specs, check_vma=False)
```

```python
import functools
import math

import jax
import jax.numpy as jnp
from jax import lax
from jax.experimental import pallas as pl
from jax.experimental.pallas import tpu as pltpu
from jax.sharding import PartitionSpec as P

HEAD_SIZE = 128
QUERY_HEADS = 16
KEY_VALUE_HEADS = 2

NEGATIVE_LIMIT = -1e30
EPSILON = 1e-06
MESH = pl.DeviceIdType.MESH


def ring_place(index, count):
    odd = index % 2
    return (1 - odd) * (index // 2) + odd * (count - 1 - index // 2)


def ring_index(place, count):
    half = place // ((count + 1) // 2)
    return (1 - half) * 2 * place + half * (2 * (count - 1 - place) + 1)


def experts_kernel(n, n_exp, tile, *refs):
    (x_ref, g_ref, up_hbm, down_hbm, out_ref) = refs[:5]
    (rows_all, gates_all, up, down, hidden, produced, arrived, summed, landed) = refs[5:14]
    (send_sem, recv_sem, peer_send, peer_recv, own_sem, w_sem) = refs[14:20]
    (fold_send, fold_recv, home_send, home_recv) = refs[20:]
    me = lax.axis_index("ctx")
    mine = lax.axis_index("exp")
    place = ring_place(me, n)
    hops = n // 2
    rows, width = x_ref.shape
    half = width // 2

    loads = [
        pltpu.make_async_copy(up_hbm, up, w_sem.at[0]),
        pltpu.make_async_copy(down_hbm, down, w_sem.at[1]),
    ]
    for copy in loads:
        copy.start()

    def source(part):
        return g_ref if part == 2 else x_ref.at[:, pl.ds(part * half, half)]

    def slot(part, index):
        if part == 2:
            return gates_all.at[index, mine]
        return rows_all.at[index, mine, :, pl.ds(part * half, half)]

    def neighbour(step):
        return ring_index((place + step + n) % n, n)

    barrier = pltpu.get_barrier_semaphore()
    for shift in range(1, n):
        pl.semaphore_signal(
            barrier, inc=1, device_id={"ctx": (me + shift) % n}, device_id_type=MESH
        )
    for shift in range(1, n_exp):
        pl.semaphore_signal(
            barrier, inc=1, device_id={"exp": (mine + shift) % n_exp}, device_id_type=MESH
        )
    pl.semaphore_wait(barrier, n - 1 + n_exp - 1)

    started = {}
    peers = []

    def pass_on(part, message, src, index):
        for shift in range(1, n_exp):
            copy = pltpu.make_async_remote_copy(
                src_ref=src,
                dst_ref=slot(part, index),
                send_sem=peer_send.at[part, message, shift - 1],
                recv_sem=peer_recv.at[part, message, shift - 1],
                device_id={"exp": (mine + shift) % n_exp},
                device_id_type=MESH,
            )
            copy.start()
            peers.append(copy)

    short = n - 1 - hops
    flows = [(0, 1, hops), (1, -1, hops), (1, 1, short), (0, -1, short), (2, 1, hops), (2, -1, short)]
    own = []
    for hop in range(1, hops + 2):
        for part, step, most in flows:
            way = (step + 1) // 2
            index = ring_index((place - step * (hop - 1) + n * hop) % n, n)
            if 1 < hop <= most + 1:
                started[part, way, hop - 1].wait_recv()
            if hop <= most:
                copy = pltpu.make_async_remote_copy(
                    src_ref=source(part) if hop == 1 else slot(part, index),
                    dst_ref=slot(part, index),
                    send_sem=send_sem.at[part, way, hop - 1],
                    recv_sem=recv_sem.at[part, way, hop - 1],
                    device_id={"ctx": neighbour(step)},
                    device_id_type=MESH,
                )
                copy.start()
                started[part, way, hop] = copy
            if 1 < hop <= most + 1:
                pass_on(part, 1 + way * hops + hop - 2, slot(part, index), index)
        if hop == 1:
            for part in range(3):
                copy = pltpu.make_async_copy(source(part), slot(part, me), own_sem.at[part])
                copy.start()
                own.append(copy)
                pass_on(part, 0, source(part), me)
    for copy in own:
        copy.wait()
    for copy in started.values():
        copy.wait_send()
    for copy in peers:
        copy.wait()
    for copy in loads:
        copy.wait()

    total = n * n_exp * rows
    units = hidden.shape[1]

    def widen(t, carry):
        at = pl.multiple_of(t * tile, tile)
        x = rows_all[...].reshape(total, width)
        gate = jnp.dot(x, up[:, pl.ds(at, tile)], preferred_element_type=jnp.float32)
        linear = jnp.dot(
            x, up[:, pl.ds(pl.multiple_of(units + at, tile), tile)],
            preferred_element_type=jnp.float32,
        )
        hidden[:, pl.ds(at, tile)] = (gate / (1.0 + jnp.exp(-gate)) * linear).astype(jnp.bfloat16)
        return carry

    lax.fori_loop(0, units // tile, widen, 0)

    def narrow(t, carry):
        at = pl.multiple_of(t * tile, tile)
        y = jnp.dot(hidden[...], down[:, pl.ds(at, tile)], preferred_element_type=jnp.float32)
        produced[:, :, :, pl.ds(at, tile)] = y.astype(jnp.bfloat16).reshape(n, n_exp, rows, tile)
        return carry

    lax.fori_loop(0, width // tile, narrow, 0)

    order = [(me + n // 2 + turn) % n for turn in range(n)]
    folds = {}
    for turn in range(n):
        for shift in range(1, n_exp):
            to = (mine + shift) % n_exp
            copy = pltpu.make_async_remote_copy(
                src_ref=produced.at[order[turn], to],
                dst_ref=arrived.at[shift - 1, turn],
                send_sem=fold_send.at[shift - 1, turn],
                recv_sem=fold_recv.at[shift - 1, turn],
                device_id={"exp": to},
                device_id_type=MESH,
            )
            copy.start()
            folds[turn, shift] = copy

    lane = lax.broadcasted_iota(jnp.int32, (rows, gates_all.shape[3]), 1)
    homes = []
    for turn in range(n):
        index = order[turn]
        gates = gates_all[index, mine]

        def gate_of(peer):
            picked = jnp.where(lane == me * n_exp + peer, gates, 0.0)
            return jnp.sum(picked, -1, keepdims=True)

        value = gate_of(mine) * produced[index, mine].astype(jnp.float32)
        for shift in range(1, n_exp):
            folds[turn, shift].wait_recv()
            giver = (mine + n_exp - shift) % n_exp
            value = value + gate_of(giver) * arrived[shift - 1, turn].astype(jnp.float32)
        if turn == n - n // 2:
            out_ref[...] = value
        else:
            summed[turn] = value.astype(jnp.bfloat16)
            copy = pltpu.make_async_remote_copy(
                src_ref=summed.at[turn],
                dst_ref=landed.at[turn],
                send_sem=home_send.at[turn],
                recv_sem=home_recv.at[turn],
                device_id={"ctx": index},
                device_id_type=MESH,
            )
            copy.start()
            homes.append((turn, copy))
    for turn, copy in homes:
        copy.wait_recv()
        out_ref[...] = out_ref[...] + landed[turn].astype(jnp.float32)
    for turn, copy in homes:
        copy.wait_send()
    for copy in folds.values():
        copy.wait_send()


def experts(normed, gates, w_gate_up, w_down, n, n_exp):
    rows, width = normed.shape
    units = w_down.shape[0]
    hops = n // 2
    wide = max(1, n_exp - 1)
    vmem = pl.BlockSpec(memory_space=pltpu.VMEM)
    hbm = pl.BlockSpec(memory_space=pl.ANY)
    dma = pltpu.SemaphoreType.DMA
    return pl.pallas_call(
        functools.partial(experts_kernel, n, n_exp, math.gcd(math.gcd(units, width), 256)),
        out_shape=jax.ShapeDtypeStruct((rows, width), jnp.float32),
        in_specs=[vmem, vmem, hbm, hbm],
        out_specs=vmem,
        scratch_shapes=[
            pltpu.VMEM((n, n_exp, rows, width), jnp.bfloat16),
            pltpu.VMEM((n, n_exp) + gates.shape, jnp.float32),
            pltpu.VMEM(w_gate_up.shape, jnp.bfloat16),
            pltpu.VMEM(w_down.shape, jnp.bfloat16),
            pltpu.VMEM((n * n_exp * rows, units), jnp.bfloat16),
            pltpu.VMEM((n, n_exp, rows, width), jnp.bfloat16),
            pltpu.VMEM((wide, n, rows, width), jnp.bfloat16),
            pltpu.VMEM((n, rows, width), jnp.bfloat16),
            pltpu.VMEM((n, rows, width), jnp.bfloat16),
            dma((3, 2, hops)),
            dma((3, 2, hops)),
            dma((3, 1 + 2 * hops, wide)),
            dma((3, 1 + 2 * hops, wide)),
            dma((3,)),
            dma((2,)),
            dma((wide, n)),
            dma((wide, n)),
            dma((n,)),
            dma((n,)),
        ],
        compiler_params=pltpu.CompilerParams(
            collective_id=1, has_side_effects=True
        ),
        name="experts",
    )(normed, gates, w_gate_up, w_down)


def ring_decode_kernel(n, local_heads, *refs):
    (k_ref, v_ref, q_ref, fk_ref, fv_ref, lengths) = refs[:6]
    k_out, v_out, attn_out = refs[6:9]
    (far_q, far_k, far_v, near_attn, send_sem, recv_sem, swap_send, swap_recv, own_sem) = refs[9:]
    group = lax.axis_index("group")
    me = lax.axis_index("ctx")
    place = ring_place(me, n)
    hops = n // 2
    group_width = QUERY_HEADS // KEY_VALUE_HEADS
    column = pl.multiple_of(me * local_heads // group_width * HEAD_SIZE, HEAD_SIZE)
    head_columns = pl.ds(column, HEAD_SIZE)
    ins, outs = (k_ref, v_ref), (k_out, v_out)
    rows = k_ref.shape[0]
    samples = q_ref.shape[0]
    factor = HEAD_SIZE ** (-0.5) * math.log2(math.e)

    def neighbour(step):
        return ring_index((place + step + n) % n, n)

    barrier = pltpu.get_barrier_semaphore()
    for step in (-1, 1):
        pl.semaphore_signal(barrier, inc=1, device_id={"ctx": neighbour(step)}, device_id_type=MESH)
    pl.semaphore_signal(barrier, inc=1, device_id={"group": 1 - group}, device_id_type=MESH)
    pl.semaphore_wait(barrier, 3)

    def swap(number, src, dst):
        return pltpu.make_async_remote_copy(
            src_ref=src,
            dst_ref=dst,
            send_sem=swap_send.at[number],
            recv_sem=swap_recv.at[number],
            device_id={"group": 1 - group},
            device_id_type=MESH,
        )

    swaps = [
        swap(0, q_ref, far_q),
        swap(1, fk_ref.at[:, head_columns], far_k),
        swap(2, fv_ref.at[:, head_columns], far_v),
    ]
    flows = [(0, 1, hops), (1, -1, hops), (1, 1, n - 1 - hops), (0, -1, n - 1 - hops)]
    started = {}

    def send(hop):
        for part, step, most in flows:
            way = (step + 1) // 2
            if 1 < hop <= most + 1:
                started[part, way, hop - 1].wait_recv()
            if hop <= most:
                index = ring_index((place - step * (hop - 1) + n * hop) % n, n)
                copy = pltpu.make_async_remote_copy(
                    src_ref=ins[part] if hop == 1 else outs[part].at[index],
                    dst_ref=outs[part].at[index],
                    send_sem=send_sem.at[part, way, hop - 1],
                    recv_sem=recv_sem.at[part, way, hop - 1],
                    device_id={"ctx": neighbour(step)},
                    device_id_type=MESH,
                )
                copy.start()
                started[part, way, hop] = copy

    send(1)
    for copy in swaps:
        copy.start()
    own = [
        pltpu.make_async_copy(ins[part], outs[part].at[me], own_sem.at[part]) for part in range(2)
    ]
    for copy in own:
        copy.start()
    length = lengths[group, 0]
    for copy in swaps:
        copy.wait()
    queries = jnp.concatenate(
        [far_q[:, h * HEAD_SIZE : (h + 1) * HEAD_SIZE] for h in range(local_heads)], 0
    )
    fresh_k = jnp.concatenate([far_k[...].astype(jnp.float32)] * local_heads, 0)
    fresh_v = jnp.concatenate([far_v[...].astype(jnp.float32)] * local_heads, 0)
    peak = jnp.sum(queries.astype(jnp.float32) * fresh_k, -1, keepdims=True) * factor
    state = (peak, jnp.ones_like(peak), fresh_v)

    def advance(state, keys, values, index):
        peak, total, weighted = state
        scores = (
            lax.dot_general(
                queries, keys, (((1,), (1,)), ((), ())), preferred_element_type=jnp.float32
            )
            * factor
        )
        keep = index * rows + lax.broadcasted_iota(jnp.int32, scores.shape, 1) < length
        scores = jnp.where(keep, scores, NEGATIVE_LIMIT)
        new_peak = jnp.maximum(peak, jnp.max(scores, -1, keepdims=True))
        rescale = jnp.exp2(peak - new_peak)
        weights = jnp.where(keep, jnp.exp2(scores - new_peak), 0.0)
        total = rescale * total + jnp.sum(weights, -1, keepdims=True)
        weighted = rescale * weighted + jnp.dot(
            weights.astype(jnp.bfloat16), values, preferred_element_type=jnp.float32
        )
        return new_peak, total, weighted

    state = advance(state, k_ref[:, head_columns], v_ref[:, head_columns], me)
    for hop in range(2, hops + 2):
        send(hop)
        steps = (1, -1) if hop - 1 <= n - 1 - hops else (1,)
        for step in steps:
            index = ring_index((place - step * (hop - 1) + n * hop) % n, n)
            state = advance(
                state, k_out[index, :, head_columns], v_out[index, :, head_columns], index
            )
    peak, total, weighted = state
    mixed = (weighted / total).astype(jnp.bfloat16)
    for h in range(local_heads):
        near_attn[:, h * HEAD_SIZE : (h + 1) * HEAD_SIZE] = mixed[h * samples : (h + 1) * samples]
    back = swap(3, near_attn, attn_out)
    back.start()
    for copy in own:
        copy.wait()
    for copy in started.values():
        copy.wait_send()
    back.wait()


def ring_decode(keys, values, query, fresh_keys, fresh_values, lengths, n):
    rows, samples = keys.shape[0], query.shape[0]
    hops = n // 2
    gathered = jax.ShapeDtypeStruct((n,) + keys.shape, keys.dtype)
    vmem = pl.BlockSpec(memory_space=pltpu.VMEM)
    return pl.pallas_call(
        functools.partial(ring_decode_kernel, n, query.shape[1] // HEAD_SIZE),
        out_shape=[gathered, gathered, jax.ShapeDtypeStruct(query.shape, jnp.bfloat16)],
        in_specs=[vmem] * 5 + [pl.BlockSpec(memory_space=pltpu.SMEM)],
        out_specs=[vmem] * 3,
        scratch_shapes=[
            pltpu.VMEM(query.shape, jnp.bfloat16),
            pltpu.VMEM((samples, HEAD_SIZE), jnp.bfloat16),
            pltpu.VMEM((samples, HEAD_SIZE), jnp.bfloat16),
            pltpu.VMEM(query.shape, jnp.bfloat16),
            pltpu.SemaphoreType.DMA((2, 2, hops)),
            pltpu.SemaphoreType.DMA((2, 2, hops)),
            pltpu.SemaphoreType.DMA((4,)),
            pltpu.SemaphoreType.DMA((4,)),
            pltpu.SemaphoreType.DMA((2,)),
        ],
        compiler_params=pltpu.CompilerParams(collective_id=0, has_side_effects=True),
        name="ring_decode",
    )(keys, values, query, fresh_keys, fresh_values, lengths)


def prefill_kernel(heads, tile, lengths, q_ref, k_ref, v_ref, out_ref, held):
    rows = q_ref.shape[0]
    lanes = HEAD_SIZE
    factor = HEAD_SIZE ** (-0.5) * math.log2(math.e)
    length = lengths[lax.axis_index("group"), 0]
    base = lax.axis_index("ctx") * rows
    limit = jnp.where(base < length, jnp.minimum(length, base + rows), 0)
    last = (limit + tile - 1) // tile
    free = jnp.minimum(jnp.minimum(length, base) // tile, last)
    queries = [q_ref[:, h * HEAD_SIZE : (h + 1) * HEAD_SIZE] for h in range(heads)]

    def score(masked, j, carry):
        start = pl.multiple_of(j * tile, tile)
        keys = k_ref[pl.ds(start, tile), :]
        if masked:
            column = start + lax.broadcasted_iota(jnp.int32, (rows, tile), 1)
            row = base + lax.broadcasted_iota(jnp.int32, (rows, tile), 0)
            keep = (column < length) & (column <= row)
        result = []
        for h in range(heads):
            scores = lax.dot_general(
                queries[h], keys, (((1,), (1,)), ((), ())), preferred_element_type=jnp.float32
            )
            if masked:
                scores = jnp.where(keep, scores, NEGATIVE_LIMIT)
            held[h, :, pl.ds(start, tile)] = scores
            peak = carry[h]
            for at in range(0, tile, lanes):
                peak = jnp.maximum(peak, scores[:, at : at + lanes])
            result.append(peak)
        return tuple(result)

    peaks = tuple(jnp.full((rows, lanes), NEGATIVE_LIMIT, jnp.float32) for h in range(heads))
    peaks = lax.fori_loop(0, free, functools.partial(score, False), peaks)
    peaks = lax.fori_loop(free, last, functools.partial(score, True), peaks)
    peaks = [
        jnp.broadcast_to(jnp.max(peak, -1, keepdims=True), (rows, lanes)) for peak in peaks
    ]

    def weigh(j, carry):
        start = pl.multiple_of(j * tile, tile)
        values = v_ref[pl.ds(start, tile), :]
        result = []
        for h in range(heads):
            total, weighted = carry[2 * h : 2 * h + 2]
            pieces = []
            for at in range(0, tile, lanes):
                scores = held[h, :, pl.ds(pl.multiple_of(start + at, lanes), lanes)]
                weights = jnp.exp2((scores - peaks[h]) * factor)
                total = total + weights
                pieces.append(weights.astype(jnp.bfloat16))
            weighted = weighted + jnp.dot(
                jnp.concatenate(pieces, -1), values, preferred_element_type=jnp.float32
            )
            result += [total, weighted]
        return tuple(result)

    zeros = jnp.zeros((rows, HEAD_SIZE), jnp.float32)
    carry = lax.fori_loop(0, last, weigh, (zeros,) * (2 * heads))
    row = base + lax.broadcasted_iota(jnp.int32, (rows, HEAD_SIZE), 0)
    for h in range(heads):
        total, weighted = carry[2 * h : 2 * h + 2]
        total = jnp.sum(total, -1, keepdims=True)
        mixed = weighted / jnp.where(total > 0, total, 1.0)
        mixed = jnp.where(row < length, mixed, 0.0)
        out_ref[:, h * HEAD_SIZE : (h + 1) * HEAD_SIZE] = mixed.astype(jnp.bfloat16)


def prefill(lengths, queries, keys, values):
    rows, width = queries.shape
    count = width // HEAD_SIZE
    group_width = QUERY_HEADS // KEY_VALUE_HEADS
    heads = math.gcd(group_width, 2)
    prompt_len = keys.shape[0]
    kv_spec = pl.BlockSpec((prompt_len, HEAD_SIZE), lambda i, info: (0, i * heads // group_width))
    q_spec = pl.BlockSpec((rows, heads * HEAD_SIZE), lambda i, info: (0, i))
    return pl.pallas_call(
        functools.partial(prefill_kernel, heads, math.gcd(prompt_len, 512)),
        out_shape=jax.ShapeDtypeStruct((rows, width), jnp.bfloat16),
        grid_spec=pltpu.PrefetchScalarGridSpec(
            num_scalar_prefetch=1,
            grid=(count // heads,),
            in_specs=[q_spec, kv_spec, kv_spec],
            out_specs=q_spec,
            scratch_shapes=[pltpu.VMEM((heads, rows, prompt_len), jnp.float32)],
        ),
        compiler_params=pltpu.CompilerParams(dimension_semantics=("arbitrary",)),
        cost_estimate=pl.CostEstimate(
            flops=4 * rows * width * prompt_len,
            bytes_accessed=4 * rows * width + 4 * prompt_len * keys.shape[1],
            transcendentals=rows * count * prompt_len,
        ),
        name="prefill",
    )(lengths, queries, keys, values)


def body(
    prompt_query,
    prompt_keys,
    prompt_values,
    lengths,
    decode_query,
    fresh_keys,
    fresh_values,
    x_dec,
    w_out,
    norm_gain,
    w_gate_up,
    w_down,
    expert_ids,
    gate_weights,
):
    n_ctx = lax.axis_size("ctx")
    n_exp = lax.axis_size("exp")
    prompt_len = prompt_query.shape[2] * n_ctx
    keys, values, dec_attn = ring_decode(
        prompt_keys[0, 0],
        prompt_values[0, 0],
        decode_query[0, 0],
        fresh_keys[0, 0],
        fresh_values[0, 0],
        lengths,
        n_ctx,
    )
    keys = keys.reshape(prompt_len, keys.shape[-1])
    values = values.reshape(prompt_len, values.shape[-1])
    row_count = x_dec.shape[2]
    shares = jnp.dot(dec_attn, w_out, preferred_element_type=jnp.float32).astype(jnp.bfloat16)
    shares = shares.reshape(n_ctx, row_count, shares.shape[1])
    keys, values, shares = lax.optimization_barrier((keys, values, shares))
    shares = lax.all_to_all(shares, "ctx", split_axis=0, concat_axis=0, tiled=True)
    prompt_attn = prefill(lengths, prompt_query[0, 0], keys, values)
    shares, prompt_attn = lax.optimization_barrier((shares, prompt_attn))
    prompt_attention = prompt_attn.reshape(prompt_query.shape)

    projected = jnp.sum(shares.astype(jnp.float32), 0)
    residual = x_dec[0, 0].astype(jnp.float32) + projected
    normed = (
        residual
        * lax.rsqrt(jnp.mean(residual * residual, -1, keepdims=True) + EPSILON)
        * norm_gain.astype(jnp.float32)
    ).astype(jnp.bfloat16)
    model_width = normed.shape[1]
    top_count = expert_ids.shape[3]
    experts_all = w_gate_up.shape[0] * n_ctx * n_exp
    capacity = min(row_count, max(2, 2 * row_count * top_count // experts_all))
    every_row = capacity == row_count
    ids = expert_ids[0, 0]
    chosen = ids[:, :, None] == lax.iota(jnp.int32, experts_all)[None, None, :]
    gate_values = gate_weights[0, 0]
    if every_row:
        gates = jnp.sum(jnp.where(chosen, gate_values[:, :, None], 0.0), 1)
        gates = jnp.pad(gates, ((0, 0), (0, -experts_all % 128)))
        moe = experts(normed, gates, w_gate_up[0], w_down[0], n_ctx, n_exp)
    else:
        one_hot = chosen.reshape(-1, experts_all).astype(jnp.int32)
        earlier = jnp.cumsum(one_hot, 0) - one_hot
        target = ids.reshape(-1) * capacity + jnp.sum(earlier * one_hot, 1)
        placing = (
            lax.iota(jnp.int32, experts_all * capacity)[:, None, None]
            == target.reshape(row_count, top_count)[None]
        ).any(-1)
        buffer = jnp.dot(
            placing.astype(jnp.bfloat16), normed, preferred_element_type=jnp.float32
        ).astype(jnp.bfloat16)
        buffer = buffer.reshape(experts_all, capacity, model_width)
        arrived = lax.all_to_all(buffer, ("ctx", "exp"), split_axis=0, concat_axis=0, tiled=True)
        flat_rows = arrived.reshape(-1, model_width)
        mixed = jnp.dot(flat_rows, w_gate_up[0], preferred_element_type=jnp.float32)
        hidden_units = mixed.shape[1] // 2
        hidden = (jax.nn.silu(mixed[:, :hidden_units]) * mixed[:, hidden_units:]).astype(
            jnp.bfloat16
        )
        produced = jnp.dot(hidden, w_down[0], preferred_element_type=jnp.float32)
        outputs = produced.astype(jnp.bfloat16).reshape(experts_all, capacity, model_width)
        returned = lax.all_to_all(outputs, ("ctx", "exp"), split_axis=0, concat_axis=0, tiled=True)
        picked = returned.reshape(experts_all * capacity, model_width)[target]
        moe = jnp.sum(
            picked.reshape(row_count, top_count, model_width).astype(jnp.float32)
            * gate_values[..., None],
            1,
        )
    out_dec = (residual + moe).astype(jnp.bfloat16).reshape(1, 1, row_count, model_width)
    return (prompt_attention, out_dec)


def solution(mesh):
    in_specs = (
        P("group", "exp", "ctx", None),
        P("group", "exp", "ctx", None),
        P("group", "exp", "ctx", None),
        P(None, "exp"),
        P("group", "exp", None, "ctx"),
        P("group", "exp", None, None),
        P("group", "exp", None, None),
        P("group", "exp", "ctx", None),
        P("ctx", None),
        P(),
        P(("ctx", "exp"), None, None),
        P(("ctx", "exp"), None, None),
        P("group", "exp", "ctx", None),
        P("group", "exp", "ctx", None),
    )
    out_specs = (P("group", "exp", "ctx", None), P("group", "exp", "ctx", None))
    return jax.shard_map(body, mesh=mesh, in_specs=in_specs, out_specs=out_specs, check_vma=False)
```

```python
import functools
import math

import jax
import jax.numpy as jnp
from jax import lax
from jax.experimental import pallas as pl
from jax.experimental.pallas import tpu as pltpu
from jax.sharding import PartitionSpec as P

HEAD_SIZE = 128
QUERY_HEADS = 16
KEY_VALUE_HEADS = 2

NEGATIVE_LIMIT = -1e30
EPSILON = 1e-06
STACK = 4
TILE = 1024
MESH = pl.DeviceIdType.MESH


def ring_place(index, count):
    odd = index % 2
    return (1 - odd) * (index // 2) + odd * (count - 1 - index // 2)


def ring_index(place, count):
    half = place // ((count + 1) // 2)
    return (1 - half) * 2 * place + half * (2 * (count - 1 - place) + 1)


def experts_kernel(n, n_exp, tile, *refs):
    (x_ref, g_ref, up_hbm, down_hbm, out_ref) = refs[:5]
    (rows_all, gates_all, up, down, hidden, produced, arrived, summed, landed) = refs[5:14]
    (send_sem, recv_sem, peer_send, peer_recv, own_sem, w_sem) = refs[14:20]
    (fold_send, fold_recv, home_send, home_recv) = refs[20:]
    me = lax.axis_index("ctx")
    mine = lax.axis_index("exp")
    place = ring_place(me, n)
    hops = n // 2
    rows, width = x_ref.shape
    half = width // 2

    loads = [
        pltpu.make_async_copy(up_hbm, up, w_sem.at[0]),
        pltpu.make_async_copy(down_hbm, down, w_sem.at[1]),
    ]
    for copy in loads:
        copy.start()

    def source(part):
        return g_ref if part == 2 else x_ref.at[:, pl.ds(part * half, half)]

    def slot(part, index):
        if part == 2:
            return gates_all.at[index, mine]
        return rows_all.at[index, mine, :, pl.ds(part * half, half)]

    def neighbour(step):
        return ring_index((place + step + n) % n, n)

    barrier = pltpu.get_barrier_semaphore()
    for shift in range(1, n):
        pl.semaphore_signal(
            barrier, inc=1, device_id={"ctx": (me + shift) % n}, device_id_type=MESH
        )
    for shift in range(1, n_exp):
        pl.semaphore_signal(
            barrier, inc=1, device_id={"exp": (mine + shift) % n_exp}, device_id_type=MESH
        )
    pl.semaphore_wait(barrier, n - 1 + n_exp - 1)

    started = {}
    peers = []

    def pass_on(part, message, src, index):
        for shift in range(1, n_exp):
            copy = pltpu.make_async_remote_copy(
                src_ref=src,
                dst_ref=slot(part, index),
                send_sem=peer_send.at[part, message, shift - 1],
                recv_sem=peer_recv.at[part, message, shift - 1],
                device_id={"exp": (mine + shift) % n_exp},
                device_id_type=MESH,
            )
            copy.start()
            peers.append(copy)

    short = n - 1 - hops
    flows = [(0, 1, hops), (1, -1, hops), (1, 1, short), (0, -1, short), (2, 1, hops), (2, -1, short)]
    own = []
    for hop in range(1, hops + 2):
        for part, step, most in flows:
            way = (step + 1) // 2
            index = ring_index((place - step * (hop - 1) + n * hop) % n, n)
            if 1 < hop <= most + 1:
                started[part, way, hop - 1].wait_recv()
            if hop <= most:
                copy = pltpu.make_async_remote_copy(
                    src_ref=source(part) if hop == 1 else slot(part, index),
                    dst_ref=slot(part, index),
                    send_sem=send_sem.at[part, way, hop - 1],
                    recv_sem=recv_sem.at[part, way, hop - 1],
                    device_id={"ctx": neighbour(step)},
                    device_id_type=MESH,
                )
                copy.start()
                started[part, way, hop] = copy
            if 1 < hop <= most + 1:
                pass_on(part, 1 + way * hops + hop - 2, slot(part, index), index)
        if hop == 1:
            for part in range(3):
                copy = pltpu.make_async_copy(source(part), slot(part, me), own_sem.at[part])
                copy.start()
                own.append(copy)
                pass_on(part, 0, source(part), me)
    for copy in own:
        copy.wait()
    for copy in started.values():
        copy.wait_send()
    for copy in peers:
        copy.wait()
    for copy in loads:
        copy.wait()

    total = n * n_exp * rows
    units = hidden.shape[1]

    def widen(t, carry):
        at = pl.multiple_of(t * tile, tile)
        x = rows_all[...].reshape(total, width)
        gate = jnp.dot(x, up[:, pl.ds(at, tile)], preferred_element_type=jnp.float32)
        linear = jnp.dot(
            x, up[:, pl.ds(pl.multiple_of(units + at, tile), tile)],
            preferred_element_type=jnp.float32,
        )
        hidden[:, pl.ds(at, tile)] = (gate / (1.0 + jnp.exp(-gate)) * linear).astype(jnp.bfloat16)
        return carry

    lax.fori_loop(0, units // tile, widen, 0)

    def narrow(t, carry):
        at = pl.multiple_of(t * tile, tile)
        y = jnp.dot(hidden[...], down[:, pl.ds(at, tile)], preferred_element_type=jnp.float32)
        produced[:, :, :, pl.ds(at, tile)] = y.astype(jnp.bfloat16).reshape(n, n_exp, rows, tile)
        return carry

    lax.fori_loop(0, width // tile, narrow, 0)

    order = [(me + n // 2 + turn) % n for turn in range(n)]
    folds = {}
    for turn in range(n):
        for shift in range(1, n_exp):
            to = (mine + shift) % n_exp
            copy = pltpu.make_async_remote_copy(
                src_ref=produced.at[order[turn], to],
                dst_ref=arrived.at[shift - 1, turn],
                send_sem=fold_send.at[shift - 1, turn],
                recv_sem=fold_recv.at[shift - 1, turn],
                device_id={"exp": to},
                device_id_type=MESH,
            )
            copy.start()
            folds[turn, shift] = copy

    lane = lax.broadcasted_iota(jnp.int32, (rows, gates_all.shape[3]), 1)
    homes = []
    for turn in range(n):
        index = order[turn]
        gates = gates_all[index, mine]

        def gate_of(peer):
            picked = jnp.where(lane == me * n_exp + peer, gates, 0.0)
            return jnp.sum(picked, -1, keepdims=True)

        value = gate_of(mine) * produced[index, mine].astype(jnp.float32)
        for shift in range(1, n_exp):
            folds[turn, shift].wait_recv()
            giver = (mine + n_exp - shift) % n_exp
            value = value + gate_of(giver) * arrived[shift - 1, turn].astype(jnp.float32)
        if turn == n - n // 2:
            out_ref[...] = value
        else:
            summed[turn] = value.astype(jnp.bfloat16)
            copy = pltpu.make_async_remote_copy(
                src_ref=summed.at[turn],
                dst_ref=landed.at[turn],
                send_sem=home_send.at[turn],
                recv_sem=home_recv.at[turn],
                device_id={"ctx": index},
                device_id_type=MESH,
            )
            copy.start()
            homes.append((turn, copy))
    for turn, copy in homes:
        copy.wait_recv()
        out_ref[...] = out_ref[...] + landed[turn].astype(jnp.float32)
    for turn, copy in homes:
        copy.wait_send()
    for copy in folds.values():
        copy.wait_send()


def experts(normed, gates, w_gate_up, w_down, n, n_exp):
    rows, width = normed.shape
    units = w_down.shape[0]
    hops = n // 2
    wide = max(1, n_exp - 1)
    vmem = pl.BlockSpec(memory_space=pltpu.VMEM)
    hbm = pl.BlockSpec(memory_space=pl.ANY)
    dma = pltpu.SemaphoreType.DMA
    return pl.pallas_call(
        functools.partial(experts_kernel, n, n_exp, math.gcd(math.gcd(units, width), 256)),
        out_shape=jax.ShapeDtypeStruct((rows, width), jnp.float32),
        in_specs=[vmem, vmem, hbm, hbm],
        out_specs=vmem,
        scratch_shapes=[
            pltpu.VMEM((n, n_exp, rows, width), jnp.bfloat16),
            pltpu.VMEM((n, n_exp) + gates.shape, jnp.float32),
            pltpu.VMEM(w_gate_up.shape, jnp.bfloat16),
            pltpu.VMEM(w_down.shape, jnp.bfloat16),
            pltpu.VMEM((n * n_exp * rows, units), jnp.bfloat16),
            pltpu.VMEM((n, n_exp, rows, width), jnp.bfloat16),
            pltpu.VMEM((wide, n, rows, width), jnp.bfloat16),
            pltpu.VMEM((n, rows, width), jnp.bfloat16),
            pltpu.VMEM((n, rows, width), jnp.bfloat16),
            dma((3, 2, hops)),
            dma((3, 2, hops)),
            dma((3, 1 + 2 * hops, wide)),
            dma((3, 1 + 2 * hops, wide)),
            dma((3,)),
            dma((2,)),
            dma((wide, n)),
            dma((wide, n)),
            dma((n,)),
            dma((n,)),
        ],
        compiler_params=pltpu.CompilerParams(
            collective_id=1, has_side_effects=True
        ),
        name="experts",
    )(normed, gates, w_gate_up, w_down)


def ring_decode_kernel(n, local_heads, *refs):
    (k_ref, v_ref, q_ref, fk_ref, fv_ref, lengths) = refs[:6]
    k_out, v_out, attn_out = refs[6:9]
    (far_q, far_k, far_v, near_attn, send_sem, recv_sem, swap_send, swap_recv, own_sem) = refs[9:]
    group = lax.axis_index("group")
    me = lax.axis_index("ctx")
    place = ring_place(me, n)
    hops = n // 2
    group_width = QUERY_HEADS // KEY_VALUE_HEADS
    column = pl.multiple_of(me * local_heads // group_width * HEAD_SIZE, HEAD_SIZE)
    head_columns = pl.ds(column, HEAD_SIZE)
    ins, outs = (k_ref, v_ref), (k_out, v_out)
    rows = k_ref.shape[0]
    samples = q_ref.shape[0]
    factor = HEAD_SIZE ** (-0.5) * math.log2(math.e)

    def neighbour(step):
        return ring_index((place + step + n) % n, n)

    barrier = pltpu.get_barrier_semaphore()
    for step in (-1, 1):
        pl.semaphore_signal(barrier, inc=1, device_id={"ctx": neighbour(step)}, device_id_type=MESH)
    pl.semaphore_signal(barrier, inc=1, device_id={"group": 1 - group}, device_id_type=MESH)
    pl.semaphore_wait(barrier, 3)

    def swap(number, src, dst):
        return pltpu.make_async_remote_copy(
            src_ref=src,
            dst_ref=dst,
            send_sem=swap_send.at[number],
            recv_sem=swap_recv.at[number],
            device_id={"group": 1 - group},
            device_id_type=MESH,
        )

    swaps = [
        swap(0, q_ref, far_q),
        swap(1, fk_ref.at[:, head_columns], far_k),
        swap(2, fv_ref.at[:, head_columns], far_v),
    ]
    flows = [(0, 1, hops), (1, -1, hops), (1, 1, n - 1 - hops), (0, -1, n - 1 - hops)]
    started = {}

    def send(hop):
        for part, step, most in flows:
            way = (step + 1) // 2
            if 1 < hop <= most + 1:
                started[part, way, hop - 1].wait_recv()
            if hop <= most:
                index = ring_index((place - step * (hop - 1) + n * hop) % n, n)
                copy = pltpu.make_async_remote_copy(
                    src_ref=ins[part] if hop == 1 else outs[part].at[index],
                    dst_ref=outs[part].at[index],
                    send_sem=send_sem.at[part, way, hop - 1],
                    recv_sem=recv_sem.at[part, way, hop - 1],
                    device_id={"ctx": neighbour(step)},
                    device_id_type=MESH,
                )
                copy.start()
                started[part, way, hop] = copy

    send(1)
    for copy in swaps:
        copy.start()
    own = [
        pltpu.make_async_copy(ins[part], outs[part].at[me], own_sem.at[part]) for part in range(2)
    ]
    for copy in own:
        copy.start()
    length = lengths[group]
    for copy in swaps:
        copy.wait()
    queries = jnp.concatenate(
        [far_q[:, h * HEAD_SIZE : (h + 1) * HEAD_SIZE] for h in range(local_heads)], 0
    )
    fresh_k = jnp.concatenate([far_k[...].astype(jnp.float32)] * local_heads, 0)
    fresh_v = jnp.concatenate([far_v[...].astype(jnp.float32)] * local_heads, 0)
    peak = jnp.sum(queries.astype(jnp.float32) * fresh_k, -1, keepdims=True) * factor
    state = (peak, jnp.ones_like(peak), fresh_v)

    def advance(state, keys, values, index):
        peak, total, weighted = state
        scores = (
            lax.dot_general(
                queries, keys, (((1,), (1,)), ((), ())), preferred_element_type=jnp.float32
            )
            * factor
        )
        keep = index * rows + lax.broadcasted_iota(jnp.int32, scores.shape, 1) < length
        scores = jnp.where(keep, scores, NEGATIVE_LIMIT)
        new_peak = jnp.maximum(peak, jnp.max(scores, -1, keepdims=True))
        rescale = jnp.exp2(peak - new_peak)
        weights = jnp.where(keep, jnp.exp2(scores - new_peak), 0.0)
        total = rescale * total + jnp.sum(weights, -1, keepdims=True)
        weighted = rescale * weighted + jnp.dot(
            weights.astype(jnp.bfloat16), values, preferred_element_type=jnp.float32
        )
        return new_peak, total, weighted

    state = advance(state, k_ref[:, head_columns], v_ref[:, head_columns], me)
    for hop in range(2, hops + 2):
        send(hop)
        steps = (1, -1) if hop - 1 <= n - 1 - hops else (1,)
        for step in steps:
            index = ring_index((place - step * (hop - 1) + n * hop) % n, n)
            state = advance(
                state, k_out[index, :, head_columns], v_out[index, :, head_columns], index
            )
    peak, total, weighted = state
    mixed = (weighted / total).astype(jnp.bfloat16)
    for h in range(local_heads):
        near_attn[:, h * HEAD_SIZE : (h + 1) * HEAD_SIZE] = mixed[h * samples : (h + 1) * samples]
    back = swap(3, near_attn, attn_out)
    back.start()
    for copy in own:
        copy.wait()
    for copy in started.values():
        copy.wait_send()
    back.wait()


def ring_decode(keys, values, query, fresh_keys, fresh_values, lengths, n):
    rows, samples = keys.shape[0], query.shape[0]
    hops = n // 2
    gathered = jax.ShapeDtypeStruct((n,) + keys.shape, keys.dtype)
    vmem = pl.BlockSpec(memory_space=pltpu.VMEM)
    return pl.pallas_call(
        functools.partial(ring_decode_kernel, n, query.shape[1] // HEAD_SIZE),
        out_shape=[gathered, gathered, jax.ShapeDtypeStruct(query.shape, jnp.bfloat16)],
        in_specs=[vmem] * 5 + [pl.BlockSpec(memory_space=pltpu.SMEM)],
        out_specs=[vmem] * 3,
        scratch_shapes=[
            pltpu.VMEM(query.shape, jnp.bfloat16),
            pltpu.VMEM((samples, HEAD_SIZE), jnp.bfloat16),
            pltpu.VMEM((samples, HEAD_SIZE), jnp.bfloat16),
            pltpu.VMEM(query.shape, jnp.bfloat16),
            pltpu.SemaphoreType.DMA((2, 2, hops)),
            pltpu.SemaphoreType.DMA((2, 2, hops)),
            pltpu.SemaphoreType.DMA((4,)),
            pltpu.SemaphoreType.DMA((4,)),
            pltpu.SemaphoreType.DMA((2,)),
        ],
        compiler_params=pltpu.CompilerParams(collective_id=0, has_side_effects=True),
        name="ring_decode",
    )(keys, values, query, fresh_keys, fresh_values, lengths)


def prefill_kernel(heads, tile, lengths, q_ref, k_ref, v_ref, out_ref, held):
    rows = q_ref.shape[0]
    lanes = HEAD_SIZE
    factor = HEAD_SIZE ** (-0.5) * math.log2(math.e)
    length = lengths[lax.axis_index("group")]
    base = lax.axis_index("ctx") * rows
    limit = jnp.where(base < length, jnp.minimum(length, base + rows), 0)
    last = (limit + tile - 1) // tile
    free = jnp.minimum(jnp.minimum(length, base) // tile, last)
    stacked = heads * rows
    queries = jnp.concatenate(
        [q_ref[:, h * HEAD_SIZE : (h + 1) * HEAD_SIZE] for h in range(heads)], 0
    )

    def score(masked, j, peak):
        start = pl.multiple_of(j * tile, tile)
        keys = k_ref[pl.ds(start, tile), :]
        scores = lax.dot_general(
            queries, keys, (((1,), (1,)), ((), ())), preferred_element_type=jnp.float32
        )
        if masked:
            column = start + lax.broadcasted_iota(jnp.int32, (rows, tile), 1)
            row = base + lax.broadcasted_iota(jnp.int32, (rows, tile), 0)
            keep = (column < length) & (column <= row)
            scores = jnp.concatenate(
                [
                    jnp.where(keep, scores[h * rows : (h + 1) * rows], NEGATIVE_LIMIT)
                    for h in range(heads)
                ],
                0,
            )
        held[:, pl.ds(start, tile)] = scores
        for at in range(0, tile, lanes):
            peak = jnp.maximum(peak, scores[:, at : at + lanes])
        return peak

    peak = jnp.full((stacked, lanes), NEGATIVE_LIMIT, jnp.float32)
    peak = lax.fori_loop(0, free, functools.partial(score, False), peak)
    peak = lax.fori_loop(free, last, functools.partial(score, True), peak)
    peak = jnp.broadcast_to(jnp.max(peak, -1, keepdims=True), (stacked, lanes))

    def weigh(j, carry):
        total, weighted = carry
        start = pl.multiple_of(j * tile, tile)
        values = v_ref[pl.ds(start, tile), :]
        pieces = []
        for at in range(0, tile, lanes):
            scores = held[:, pl.ds(pl.multiple_of(start + at, lanes), lanes)]
            weights = jnp.exp2((scores - peak) * factor)
            total = total + weights
            pieces.append(weights.astype(jnp.bfloat16))
        weighted = weighted + jnp.dot(
            jnp.concatenate(pieces, -1), values, preferred_element_type=jnp.float32
        )
        return total, weighted

    zeros = jnp.zeros((stacked, HEAD_SIZE), jnp.float32)
    totals, mixes = lax.fori_loop(0, last, weigh, (zeros, zeros))
    row = base + lax.broadcasted_iota(jnp.int32, (rows, HEAD_SIZE), 0)
    for h in range(heads):
        total = jnp.sum(totals[h * rows : (h + 1) * rows], -1, keepdims=True)
        mixed = mixes[h * rows : (h + 1) * rows] / jnp.where(total > 0, total, 1.0)
        mixed = jnp.where(row < length, mixed, 0.0)
        out_ref[:, h * HEAD_SIZE : (h + 1) * HEAD_SIZE] = mixed.astype(jnp.bfloat16)


def prefill(lengths, queries, keys, values):
    rows, width = queries.shape
    count = width // HEAD_SIZE
    group_width = QUERY_HEADS // KEY_VALUE_HEADS
    heads = math.gcd(group_width, STACK)
    prompt_len = keys.shape[0]
    kv_spec = pl.BlockSpec((prompt_len, HEAD_SIZE), lambda i, info: (0, i * heads // group_width))
    q_spec = pl.BlockSpec((rows, heads * HEAD_SIZE), lambda i, info: (0, i))
    return pl.pallas_call(
        functools.partial(prefill_kernel, heads, math.gcd(prompt_len, TILE)),
        out_shape=jax.ShapeDtypeStruct((rows, width), jnp.bfloat16),
        grid_spec=pltpu.PrefetchScalarGridSpec(
            num_scalar_prefetch=1,
            grid=(count // heads,),
            in_specs=[q_spec, kv_spec, kv_spec],
            out_specs=q_spec,
            scratch_shapes=[pltpu.VMEM((heads * rows, prompt_len), jnp.float32)],
        ),
        compiler_params=pltpu.CompilerParams(dimension_semantics=("arbitrary",)),
        cost_estimate=pl.CostEstimate(
            flops=4 * rows * width * prompt_len,
            bytes_accessed=4 * rows * width + 4 * prompt_len * keys.shape[1],
            transcendentals=rows * count * prompt_len,
        ),
        name="prefill",
    )(lengths, queries, keys, values)


def body(
    prompt_query,
    prompt_keys,
    prompt_values,
    lengths,
    decode_query,
    fresh_keys,
    fresh_values,
    x_dec,
    w_out,
    norm_gain,
    w_gate_up,
    w_down,
    expert_ids,
    gate_weights,
):
    n_ctx = lax.axis_size("ctx")
    n_exp = lax.axis_size("exp")
    prompt_len = prompt_query.shape[2] * n_ctx
    keys, values, dec_attn = ring_decode(
        prompt_keys[0, 0],
        prompt_values[0, 0],
        decode_query[0, 0],
        fresh_keys[0, 0],
        fresh_values[0, 0],
        lengths[:, 0],
        n_ctx,
    )
    keys = keys.reshape(prompt_len, keys.shape[-1])
    values = values.reshape(prompt_len, values.shape[-1])
    row_count = x_dec.shape[2]
    shares = jnp.dot(dec_attn, w_out, preferred_element_type=jnp.float32).astype(jnp.bfloat16)
    shares = shares.reshape(n_ctx, row_count, shares.shape[1])
    keys, values, shares = lax.optimization_barrier((keys, values, shares))
    shares = lax.all_to_all(shares, "ctx", split_axis=0, concat_axis=0, tiled=True)
    prompt_attn = prefill(lengths[:, 0], prompt_query[0, 0], keys, values)
    shares, prompt_attn = lax.optimization_barrier((shares, prompt_attn))
    prompt_attention = prompt_attn.reshape(prompt_query.shape)

    projected = jnp.sum(shares.astype(jnp.float32), 0)
    residual = x_dec[0, 0].astype(jnp.float32) + projected
    normed = (
        residual
        * lax.rsqrt(jnp.mean(residual * residual, -1, keepdims=True) + EPSILON)
        * norm_gain.astype(jnp.float32)
    ).astype(jnp.bfloat16)
    model_width = normed.shape[1]
    top_count = expert_ids.shape[3]
    experts_all = w_gate_up.shape[0] * n_ctx * n_exp
    capacity = min(row_count, max(2, 2 * row_count * top_count // experts_all))
    every_row = capacity == row_count
    ids = expert_ids[0, 0]
    chosen = ids[:, :, None] == lax.iota(jnp.int32, experts_all)[None, None, :]
    gate_values = gate_weights[0, 0]
    if every_row:
        gates = jnp.sum(jnp.where(chosen, gate_values[:, :, None], 0.0), 1)
        gates = jnp.pad(gates, ((0, 0), (0, -experts_all % 128)))
        moe = experts(normed, gates, w_gate_up[0], w_down[0], n_ctx, n_exp)
    else:
        one_hot = chosen.reshape(-1, experts_all).astype(jnp.int32)
        earlier = jnp.cumsum(one_hot, 0) - one_hot
        target = ids.reshape(-1) * capacity + jnp.sum(earlier * one_hot, 1)
        placing = (
            lax.iota(jnp.int32, experts_all * capacity)[:, None, None]
            == target.reshape(row_count, top_count)[None]
        ).any(-1)
        buffer = jnp.dot(
            placing.astype(jnp.bfloat16), normed, preferred_element_type=jnp.float32
        ).astype(jnp.bfloat16)
        buffer = buffer.reshape(experts_all, capacity, model_width)
        arrived = lax.all_to_all(buffer, ("ctx", "exp"), split_axis=0, concat_axis=0, tiled=True)
        flat_rows = arrived.reshape(-1, model_width)
        mixed = jnp.dot(flat_rows, w_gate_up[0], preferred_element_type=jnp.float32)
        hidden_units = mixed.shape[1] // 2
        hidden = (jax.nn.silu(mixed[:, :hidden_units]) * mixed[:, hidden_units:]).astype(
            jnp.bfloat16
        )
        produced = jnp.dot(hidden, w_down[0], preferred_element_type=jnp.float32)
        outputs = produced.astype(jnp.bfloat16).reshape(experts_all, capacity, model_width)
        returned = lax.all_to_all(outputs, ("ctx", "exp"), split_axis=0, concat_axis=0, tiled=True)
        picked = returned.reshape(experts_all * capacity, model_width)[target]
        moe = jnp.sum(
            picked.reshape(row_count, top_count, model_width).astype(jnp.float32)
            * gate_values[..., None],
            1,
        )
    out_dec = (residual + moe).astype(jnp.bfloat16).reshape(1, 1, row_count, model_width)
    return (prompt_attention, out_dec)


def solution(mesh):
    in_specs = (
        P("group", "exp", "ctx", None),
        P("group", "exp", "ctx", None),
        P("group", "exp", "ctx", None),
        P(None, "exp"),
        P("group", "exp", None, "ctx"),
        P("group", "exp", None, None),
        P("group", "exp", None, None),
        P("group", "exp", "ctx", None),
        P("ctx", None),
        P(),
        P(("ctx", "exp"), None, None),
        P(("ctx", "exp"), None, None),
        P("group", "exp", "ctx", None),
        P("group", "exp", "ctx", None),
    )
    out_specs = (P("group", "exp", "ctx", None), P("group", "exp", "ctx", None))
    return jax.shard_map(body, mesh=mesh, in_specs=in_specs, out_specs=out_specs, check_vma=False)
```
